256 devices in a mesh: tm: 4 (over x_lo, core), freq: 64 (over y, x_hi, z).
Axes of the slice: x: 4 (x_hi: 2, x_lo: 2; x = x_hi * 2 + x_lo), y: 4, z: 8, core: 2. Of those that a mesh axis runs over, the one named last changes fastest.
Arguments:
- visibilities: float32 [2, 4, 32, 64, 2016], P(None, None, 'tm', 'freq'), may hold values from -48 to 48
- sky_model: float32 [2, 4, 32, 64, 2016], P(None, None, 'tm', 'freq'), may hold values from -3 to 3
- gain_time: float32 [2, 2, 8, 64], P(None, None, 'tm'), may hold values from -4 to 4
- gain_band: float32 [2, 2, 64, 64], P(None, None, 'freq'), may hold values from -2.5 to 2.5
- delay_start: float32 [2, 64], replicated, may hold values from -2.2 to 2.2
- first_antenna: int32 [2016], replicated, may hold values from 0 to 63, as said below
- second_antenna: int32 [2016], replicated, may hold values from 0 to 63
Outputs:
- solved_time: float32 [2, 2, 8, 64], P(None, None, 'tm')
- solved_band: float32 [2, 2, 64, 64], P(None, None, 'freq')
- solved_delay: float32 [2, 64], replicated
- weights: float32 [32, 2016], P('tm')
- residual: float32 [2, 4, 32, 64, 2016], P(None, None, 'tm', 'freq')
The draws below stay inside these ranges and needn't reach their ends.
Inputs may be any that keep to these rules, and one draw needn't show every extreme that they name: first_antenna and second_antenna together name every unordered pair of distinct antennas of the 64 exactly once, in an order and orientation drawn from the seed.
All inputs are finite; a program needn't handle non-finite values.
Results may differ from the reference program's by a relative error of at most 0.00013.
Values sent between devices are 32-bit elements; how exact they have to be, the bound alone decides.
No kernel may reach another device: no remote copies, remote signals or barrier semaphores. Data moves between devices by JAX's collectives and lax.ppermute only.
A program may use at most 64 MiB of HBM per device.

```python
import math
import jax
import jax.numpy as jnp
import numpy as np
from jax import lax

ANTENNA_COUNT = 64
BL = 2016
INTERVAL_TIMES = 4
SWEEPS = 2
TIMES = 32
CHANNEL_COUNT = 64
INTERVAL_COUNT = 8


def clipped_values(key, dims):
    return jax.random.truncated_normal(key, -3.0, 3.0, dims, jnp.float32)


def polar_complex(amplitude, angles):
    return jnp.stack([amplitude * jnp.cos(angles), amplitude * jnp.sin(angles)])


def product_drawn(former, latter):
    return jnp.stack([former[0] * latter[0] - former[1] * latter[1], former[0] * latter[1] + former[1] * latter[0]])


def observation(key):
    split_keys = [jax.random.fold_in(key, 7100 + number) for number in range(16)]
    smaller_antenna, larger_antenna = np.triu_indices(ANTENNA_COUNT, 1)
    ordering = jax.random.permutation(split_keys[0], BL)
    swapped = jax.random.randint(split_keys[1], (BL,), 0, 2)
    lesser_ids = jnp.asarray(smaller_antenna, jnp.int32)[ordering]
    greater_ids = jnp.asarray(larger_antenna, jnp.int32)[ordering]
    first_antenna = jnp.where(swapped == 1, greater_ids, lesser_ids)
    second_antenna = jnp.where(swapped == 1, lesser_ids, greater_ids)
    time_magnitude = jnp.exp(0.2 * clipped_values(split_keys[2], (2, INTERVAL_COUNT, ANTENNA_COUNT)))
    time_phases = jax.random.uniform(split_keys[3], (2, INTERVAL_COUNT, ANTENNA_COUNT), jnp.float32, -math.pi, math.pi)
    bandpass_magnitude = jnp.exp(0.15 * clipped_values(split_keys[4], (2, CHANNEL_COUNT, ANTENNA_COUNT)))
    bandpass_phases = 0.6 * clipped_values(split_keys[5], (2, CHANNEL_COUNT, ANTENNA_COUNT))
    actual_delay = jax.random.uniform(split_keys[6], (2, ANTENNA_COUNT), jnp.float32, -2.0, 2.0)
    initial_time_gain = polar_complex(time_magnitude * jnp.exp(0.25 * clipped_values(split_keys[7], (2, INTERVAL_COUNT, ANTENNA_COUNT))), time_phases + 0.3 * clipped_values(split_keys[8], (2, INTERVAL_COUNT, ANTENNA_COUNT)))
    initial_bandpass = polar_complex(bandpass_magnitude * jnp.exp(0.15 * clipped_values(split_keys[9], (2, CHANNEL_COUNT, ANTENNA_COUNT))), bandpass_phases + 0.3 * clipped_values(split_keys[10], (2, CHANNEL_COUNT, ANTENNA_COUNT)))
    initial_delay = actual_delay + jax.random.uniform(split_keys[11], (2, ANTENNA_COUNT), jnp.float32, -0.15, 0.15)
    frequency = (jnp.arange(CHANNEL_COUNT, dtype=jnp.float32) + 0.5) / CHANNEL_COUNT - 0.5
    amplitude = jnp.repeat(time_magnitude, INTERVAL_TIMES, axis=1)[:, :, None, :] * bandpass_magnitude[:, None]
    angles = jnp.repeat(time_phases, INTERVAL_TIMES, axis=1)[:, :, None, :] + bandpass_phases[:, None] + 2.0 * math.pi * actual_delay[:, None, None, :] * frequency[None, None, :, None]
    left_amplitude = amplitude[..., first_antenna]
    right_amplitude = amplitude[..., second_antenna]
    left_angles = angles[..., first_antenna]
    right_angles = angles[..., second_antenna]
    corruption = polar_complex(left_amplitude[:, None] * right_amplitude[None], left_angles[:, None] - right_angles[None])
    cells = (2, 2, 2, TIMES, CHANNEL_COUNT, BL)
    sky_cells = clipped_values(split_keys[12], cells)
    noise = clipped_values(split_keys[13], cells)
    by_baseline = jnp.exp(jax.random.uniform(split_keys[14], (BL,), jnp.float32, 0.0, math.log(10.0)))
    by_time = jnp.exp(jax.random.uniform(split_keys[15], (TIMES,), jnp.float32, 0.0, math.log(3.0)))
    by_channel = 1.0 + 2.0 * jnp.arange(CHANNEL_COUNT, dtype=jnp.float32) / (CHANNEL_COUNT - 1)
    level = 0.02 * by_time[:, None, None] * by_channel[None, :, None] * by_baseline[None, None, :]
    observed = product_drawn(corruption, sky_cells) + noise * level
    return {'visibilities': observed.reshape(2, 4, TIMES, CHANNEL_COUNT, BL), 'sky_model': sky_cells.reshape(2, 4, TIMES, CHANNEL_COUNT, BL), 'gain_time': initial_time_gain, 'gain_band': initial_bandpass, 'delay_start': initial_delay, 'antenna_one': first_antenna, 'antenna_two': second_antenna}


def draw_visibilities(key, part):
    return observation(key)['visibilities']


def draw_sky_model(key, part):
    return observation(key)['sky_model']


def draw_gain_time(key, part):
    return observation(key)['gain_time']


def draw_gain_band(key, part):
    return observation(key)['gain_band']


def draw_delay_start(key, part):
    return observation(key)['delay_start']


def draw_first_antenna(key, part):
    return observation(key)['antenna_one']


def draw_second_antenna(key, part):
    return observation(key)['antenna_two']


def setup_inputs(seed: int = 0) -> dict:
    keys = jax.random.split(jax.random.key(seed), 8)
    visibilities = draw_visibilities(jax.random.fold_in(keys[7], 71), 0)
    sky_model = draw_sky_model(jax.random.fold_in(keys[7], 71), 0)
    gain_time = draw_gain_time(jax.random.fold_in(keys[7], 71), 0)
    gain_band = draw_gain_band(jax.random.fold_in(keys[7], 71), 0)
    delay_start = draw_delay_start(jax.random.fold_in(keys[7], 71), 0)
    first_antenna = draw_first_antenna(jax.random.fold_in(keys[7], 71), 0)
    second_antenna = draw_second_antenna(jax.random.fold_in(keys[7], 71), 0)
    return dict(visibilities=visibilities, sky_model=sky_model, gain_time=gain_time, gain_band=gain_band, delay_start=delay_start, first_antenna=first_antenna, second_antenna=second_antenna)


FULL_TURN = 2.0 * math.pi
DAMPING = 0.5
EPSILON = 1e-6
PRECISE = lax.Precision.HIGHEST


def product(former, latter):
    return jnp.stack([former[0] * latter[0] - former[1] * latter[1], former[0] * latter[1] + former[1] * latter[0]])


def conjugate(value_array):
    return jnp.stack([value_array[0], -value_array[1]])


def magnitude(value_array):
    return value_array[0] * value_array[0] + value_array[1] * value_array[1]


def selector_mask(antennas, number):
    return (antennas[:, None] == jnp.arange(number, dtype=jnp.int32)[None, :]).astype(jnp.float32)


def to_antennas(value_array, gather_table):
    leading = value_array.shape[:-1]
    flattened = value_array.reshape(-1, value_array.shape[-1])
    summed = jnp.dot(flattened, gather_table, precision=PRECISE, preferred_element_type=jnp.float32)
    return summed.reshape(leading + (gather_table.shape[1],))


def chain_gains(gain_row_stack, bandpass, delays, frequency):
    angles = FULL_TURN * delays[:, None, :] * frequency[None, :, None]
    phasor = jnp.stack([jnp.cos(angles), jnp.sin(angles)])
    band_delay = product(bandpass, phasor)
    combined_gain = product(gain_row_stack[:, :, :, None], band_delay[:, :, None])
    return combined_gain, band_delay, phasor


def evaluate(visibilities, sky_model, gain_row_stack, bandpass, delays, frequency, first_antenna, second_antenna, first_gather, second_gather, weights, purpose):
    combined_gain, band_delay, phasor = chain_gains(gain_row_stack, bandpass, delays, frequency)
    cells = (2, 2, 2) + visibilities.shape[2:]
    observed = visibilities.reshape(cells)
    sky_cells = sky_model.reshape(cells)
    left_side_gain = jnp.take(combined_gain, first_antenna, axis=-1)[:, :, None]
    right_side_gain = jnp.take(combined_gain, second_antenna, axis=-1)[:, None]
    partial_value = product(left_side_gain, sky_cells)
    predicted = product(partial_value, conjugate(right_side_gain))
    residual = observed - predicted
    if purpose == "residual":
        return residual.reshape(visibilities.shape)
    if purpose == "noise":
        return magnitude(residual).sum(axis=(0, 1, 3))
    weighted = weights[:, None, :]
    if purpose == "delay":
        turning = FULL_TURN * frequency[:, None]
        crossed = predicted[0] * residual[1] - predicted[1] * residual[0]
        numerator_terms = weighted * turning * crossed
        denominator_terms = weighted * turning * turning * magnitude(predicted)
        numerator = to_antennas(numerator_terms.sum(axis=1), first_gather) - to_antennas(numerator_terms.sum(axis=0), second_gather)
        denominator = to_antennas(denominator_terms.sum(axis=1), first_gather) + to_antennas(denominator_terms.sum(axis=0), second_gather)
        return numerator, denominator
    if purpose == "time":
        remaining_terms = jnp.broadcast_to(band_delay[:, :, None], combined_gain.shape)
    else:
        remaining_terms = product(gain_row_stack[:, :, :, None], phasor[:, :, None])
    remaining_left = jnp.take(remaining_terms, first_antenna, axis=-1)[:, :, None]
    remaining_right = jnp.take(remaining_terms, second_antenna, axis=-1)[:, None]
    forward = product(remaining_left, product(sky_cells, conjugate(right_side_gain)))
    backward = product(conjugate(partial_value), remaining_right)
    lead_terms = weighted * product(conjugate(forward), residual)
    trail_terms = weighted * conjugate(product(backward, residual))
    lead_power = weighted * magnitude(forward)
    trail_power = weighted * magnitude(backward)
    numerator = to_antennas(lead_terms.sum(axis=2), first_gather) + to_antennas(trail_terms.sum(axis=1), second_gather)
    denominator = to_antennas(lead_power.sum(axis=1), first_gather) + to_antennas(trail_power.sum(axis=0), second_gather)
    return numerator, denominator


def reference(visibilities, sky_model, gain_time, gain_band, delay_start, first_antenna, second_antenna):
    first_gather = selector_mask(first_antenna, ANTENNA_COUNT)
    second_gather = selector_mask(second_antenna, ANTENNA_COUNT)
    frequency = (jnp.arange(CHANNEL_COUNT, dtype=jnp.int32).astype(jnp.float32) + 0.5) / CHANNEL_COUNT - 0.5

    def sweep_data(purpose, solved_time, solved_band, solved_delay, weights):
        def per_interval(interval):
            observed = lax.dynamic_slice_in_dim(visibilities, interval * INTERVAL_TIMES, INTERVAL_TIMES, 2)
            sky_cells = lax.dynamic_slice_in_dim(sky_model, interval * INTERVAL_TIMES, INTERVAL_TIMES, 2)
            column_index = lax.dynamic_slice_in_dim(solved_time, interval, 1, 2)
            gain_row_stack = jnp.broadcast_to(column_index, (2, 2, INTERVAL_TIMES, ANTENNA_COUNT))
            weight_rows = lax.dynamic_slice_in_dim(weights, interval * INTERVAL_TIMES, INTERVAL_TIMES, 0)
            result = evaluate(observed, sky_cells, gain_row_stack, solved_band, solved_delay, frequency, first_antenna, second_antenna, first_gather, second_gather, weight_rows, purpose)
            if purpose == "time":
                return result[0].sum(axis=(2, 3)), result[1].sum(axis=(1, 2))
            if purpose == "band":
                return result[0].sum(axis=2), result[1].sum(axis=1)
            if purpose == "delay":
                return result[0].sum(axis=(1, 2)), result[1].sum(axis=(1, 2))
            return result

        return lax.map(per_interval, jnp.arange(INTERVAL_COUNT, dtype=jnp.int32))

    solved_time, solved_band, solved_delay = gain_time, gain_band, delay_start
    weights = jnp.ones((TIMES, BL), jnp.float32)
    for repeat in range(SWEEPS):
        noise_power = sweep_data("noise", solved_time, solved_band, solved_delay, weights).reshape(TIMES, BL)
        weights = 1.0 / (noise_power / (4 * CHANNEL_COUNT) + EPSILON)
        numerator, denominator = sweep_data("time", solved_time, solved_band, solved_delay, weights)
        numerator = jnp.moveaxis(numerator, 0, 2)
        denominator = jnp.moveaxis(denominator, 0, 1)
        solved_time = solved_time + DAMPING * numerator / denominator
        numerator, denominator = sweep_data("band", solved_time, solved_band, solved_delay, weights)
        solved_band = solved_band + DAMPING * numerator.sum(axis=0) / denominator.sum(axis=0)
        numerator, denominator = sweep_data("delay", solved_time, solved_band, solved_delay, weights)
        solved_delay = solved_delay + DAMPING * numerator.sum(axis=0) / denominator.sum(axis=0)
    blocks = sweep_data("residual", solved_time, solved_band, solved_delay, weights)
    residual = jnp.moveaxis(blocks, 0, 2).reshape(2, 4, TIMES, CHANNEL_COUNT, BL)
    return solved_time, solved_band, solved_delay, weights, residual
```

```python
import math

import jax
import jax.numpy as jnp
from jax import lax
from jax.sharding import Mesh
from jax.sharding import PartitionSpec as P

INTERVAL_TIMES = 4
SWEEPS = 2
FREQ = ("freq_0", "freq_1", "freq_2")
TM = ("tm_0", "tm_1")


FULL_TURN = 2.0 * math.pi
DAMPING = 0.5
EPSILON = 1e-06
PRECISE = lax.Precision.HIGHEST


def copy_for_each(array, axis):
    devices = lax.axis_size(axis)
    return lax.all_to_all(
        jnp.broadcast_to(array[None], (devices, *array.shape)), axis, 0, 0, tiled=True
    )


def of_everyone(array, axis):
    return copy_for_each(array, axis).sum(axis=0)


def packed_total(arrays, axis):
    flat, at, gathered = (jnp.concatenate([a.reshape(-1) for a in arrays]), 0, [])
    running = of_everyone(flat, axis)
    for a in arrays:
        gathered.append(running[at : at + a.size].reshape(a.shape))
        at += a.size
    return tuple(gathered)


def spread_total(array, axis):
    devices = lax.axis_size(axis)
    flat = array.reshape(devices, -1)
    parts = lax.all_to_all(flat, axis, 0, 0, tiled=True)
    mine = parts.sum(axis=0)
    return copy_for_each(mine, axis).reshape(array.shape)


def swap_total(array, axes):
    for axis in axes:
        array = array + lax.ppermute(array, axis, [(0, 1), (1, 0)])
    return array


def product(former, latter):
    return jnp.stack(
        [
            former[0] * latter[0] - former[1] * latter[1],
            former[0] * latter[1] + former[1] * latter[0],
        ]
    )


def conjugate(value_array):
    return jnp.stack([value_array[0], -value_array[1]])


def magnitude(value_array):
    return value_array[0] * value_array[0] + value_array[1] * value_array[1]


def selector_mask(antennas, number):
    return (antennas[:, None] == jnp.arange(number, dtype=jnp.int32)[None, :]).astype(jnp.float32)


def antenna_to_baseline(value_array, gather_table):
    leading = value_array.shape[:-1]
    flattened = value_array.reshape(-1, value_array.shape[-1])
    spread_out = jnp.dot(
        flattened, gather_table.T, precision=PRECISE, preferred_element_type=jnp.float32
    )
    return spread_out.reshape(leading + (gather_table.shape[0],))


def to_antennas(value_array, gather_table):
    leading = value_array.shape[:-1]
    flattened = value_array.reshape(-1, value_array.shape[-1])
    summed = jnp.dot(flattened, gather_table, precision=PRECISE, preferred_element_type=jnp.float32)
    return summed.reshape(leading + (gather_table.shape[1],))


def chain_gains(gain_row_stack, bandpass, delays, frequency):
    angles = FULL_TURN * delays[:, None, :] * frequency[None, :, None]
    phasor = jnp.stack([jnp.cos(angles), jnp.sin(angles)])
    band_delay = product(bandpass, phasor)
    combined_gain = product(gain_row_stack[:, :, :, None], band_delay[:, :, None])
    return (combined_gain, band_delay, phasor)


def evaluate(
    visibilities,
    sky_model,
    gain_row_stack,
    bandpass,
    delays,
    frequency,
    first_gather,
    second_gather,
    weights,
    purpose,
):
    combined_gain, band_delay, phasor = chain_gains(gain_row_stack, bandpass, delays, frequency)
    cells = (2, 2, 2) + visibilities.shape[2:]
    observed = visibilities.reshape(cells)
    sky_cells = sky_model.reshape(cells)
    left_side_gain = antenna_to_baseline(combined_gain, first_gather)[:, :, None]
    right_side_gain = antenna_to_baseline(combined_gain, second_gather)[:, None]
    partial_value = product(left_side_gain, sky_cells)
    predicted = product(partial_value, conjugate(right_side_gain))
    residual = observed - predicted
    if purpose == "residual":
        return residual.reshape(visibilities.shape)
    if purpose == "noise":
        return magnitude(residual).sum(axis=(0, 1, 3))
    weighted = weights[:, None, :]
    if purpose == "delay":
        turning = FULL_TURN * frequency[:, None]
        crossed = predicted[0] * residual[1] - predicted[1] * residual[0]
        numerator_terms = weighted * turning * crossed
        denominator_terms = weighted * turning * turning * magnitude(predicted)
        numerator = to_antennas(numerator_terms.sum(axis=1), first_gather) - to_antennas(
            numerator_terms.sum(axis=0), second_gather
        )
        denominator = to_antennas(denominator_terms.sum(axis=1), first_gather) + to_antennas(
            denominator_terms.sum(axis=0), second_gather
        )
        return (numerator, denominator)
    if purpose == "time":
        remaining_terms = jnp.broadcast_to(band_delay[:, :, None], combined_gain.shape)
    else:
        remaining_terms = product(gain_row_stack[:, :, :, None], phasor[:, :, None])
    remaining_left = antenna_to_baseline(remaining_terms, first_gather)[:, :, None]
    remaining_right = antenna_to_baseline(remaining_terms, second_gather)[:, None]
    forward = product(remaining_left, product(sky_cells, conjugate(right_side_gain)))
    backward = product(conjugate(partial_value), remaining_right)
    lead_terms = weighted * product(conjugate(forward), residual)
    trail_terms = weighted * conjugate(product(backward, residual))
    lead_power = weighted * magnitude(forward)
    trail_power = weighted * magnitude(backward)
    numerator = to_antennas(lead_terms.sum(axis=2), first_gather) + to_antennas(
        trail_terms.sum(axis=1), second_gather
    )
    denominator = to_antennas(lead_power.sum(axis=1), first_gather) + to_antennas(
        trail_power.sum(axis=0), second_gather
    )
    return (numerator, denominator)


def shards(
    visibilities, sky_model, gain_time, gain_band, delay_start, first_antenna, second_antenna
):
    antennas = gain_time.shape[-1]
    first_gather = selector_mask(first_antenna, antennas)
    second_gather = selector_mask(second_antenna, antennas)
    local_channels = visibilities.shape[3]
    channels = local_channels * lax.axis_size(FREQ)
    offset = lax.axis_index(FREQ) * local_channels
    frequency = (offset + jnp.arange(local_channels, dtype=jnp.int32)).astype(jnp.float32)
    frequency = (frequency + 0.5) / channels - 0.5
    local_times = visibilities.shape[2]
    intervals = local_times // INTERVAL_TIMES
    solved_time, solved_band, solved_delay = (gain_time, gain_band, delay_start)
    weights = jnp.ones((local_times, visibilities.shape[4]), jnp.float32)

    def measure(purpose, current_time, current_band, current_delay, current_weights):
        gain_row_stack = jnp.repeat(current_time, INTERVAL_TIMES, axis=2)
        return evaluate(
            visibilities,
            sky_model,
            gain_row_stack,
            current_band,
            current_delay,
            frequency,
            first_gather,
            second_gather,
            current_weights,
            purpose,
        )

    for repeat in range(SWEEPS):
        noise_power = measure("noise", solved_time, solved_band, solved_delay, weights)
        summed = spread_total(noise_power, FREQ)
        weights = 1.0 / (summed / (4 * channels) + EPSILON)
        numerator, denominator = measure("time", solved_time, solved_band, solved_delay, weights)
        numerator = (
            numerator.sum(axis=3).reshape(2, 2, intervals, INTERVAL_TIMES, antennas).sum(axis=3)
        )
        denominator = (
            denominator.sum(axis=2).reshape(2, intervals, INTERVAL_TIMES, antennas).sum(axis=2)
        )
        numerator, denominator = packed_total((numerator, denominator), FREQ)
        solved_time = solved_time + DAMPING * numerator / denominator
        numerator, denominator = measure("band", solved_time, solved_band, solved_delay, weights)
        packed = jnp.concatenate(
            [numerator.sum(axis=2).reshape(-1), denominator.sum(axis=1).reshape(-1)]
        )
        packed = swap_total(packed, ("tm_1", "tm_0"))
        numerator = packed[: solved_band.size].reshape(solved_band.shape)
        denominator = packed[solved_band.size :].reshape(solved_band.shape[1:])
        solved_band = solved_band + DAMPING * numerator / denominator
        numerator, denominator = measure("delay", solved_time, solved_band, solved_delay, weights)
        packed = jnp.stack([numerator.sum(axis=(1, 2)), denominator.sum(axis=(1, 2))])
        packed = swap_total(of_everyone(packed, FREQ), ("tm_1", "tm_0"))
        numerator, denominator = packed[0], packed[1]
        solved_delay = solved_delay + DAMPING * numerator / denominator
    residual = measure("residual", solved_time, solved_band, solved_delay, weights)
    return (solved_time, solved_band, solved_delay, weights, residual)


def solution(mesh):
    split = Mesh(
        mesh.devices.reshape(2, 2, 4, 2, 8), ("tm_0", "tm_1", "freq_0", "freq_1", "freq_2")
    )
    placed = (
        P(None, None, TM, FREQ, None),
        P(None, None, TM, FREQ, None),
        P(None, None, TM, None),
        P(None, None, FREQ, None),
        P(),
        P(),
        P(),
    )
    return jax.shard_map(
        shards,
        mesh=split,
        in_specs=placed,
        out_specs=(
            P(None, None, TM, None),
            P(None, None, FREQ, None),
            P(),
            P(TM, None),
            P(None, None, TM, FREQ, None),
        ),
        check_vma=False,
    )
```

```python
import functools
import math

import jax
import jax.numpy as jnp
from jax import lax
from jax.experimental import pallas as pl
from jax.experimental.pallas import tpu as pltpu
from jax.sharding import Mesh
from jax.sharding import PartitionSpec as P

SWEEPS = 2
TURN = 2.0 * math.pi
DAMPING = 0.5
EPSILON = 1e-06
LANES = 128
HALF = 64
FREQ = ("freq_0", "freq_1", "freq_2")
TM = ("tm_0", "tm_1")
F32 = jnp.float32


def rows_of(array, start, count):
    return array[start : start + count]


def half_roll(array):
    return pltpu.roll(array, HALF, 1)


def low_half(shape):
    return lax.broadcasted_iota(jnp.int32, shape, 1) < HALF


def cmul(ar, ai, br, bi):
    return ar * br - ai * bi, ar * bi + ai * br


def conj_mul(ar, ai, br, bi):
    return ar * br + ai * bi, ar * bi - ai * br


def chain(gain, band, delay, x):
    angle = TURN * delay * x
    kr, ki = jnp.cos(angle), jnp.sin(angle)
    hr, hi = cmul(band[0:2], band[2:4], kr, ki)
    gr, gi = cmul(gain[0:2], gain[2:4], hr, hi)
    return (kr, ki), (hr, hi), (gr, gi)


def fill(row):
    return jnp.broadcast_to(row, (8, LANES))


def index_rows(index_ref, side, block, offset):
    row = index_ref[side : side + 1, block * LANES : (block + 1) * LANES]
    return fill(row) + offset


def lookup(source, index):
    return jnp.take_along_axis(source, index, axis=1)


def residual_blocks(v_ref, s_ref, index_ref, gr, gi):
    offset = jnp.where(lax.broadcasted_iota(jnp.int32, (8, LANES), 0) >= 4, HALF, 0)
    sources = [(fill(gr[a : a + 1]), fill(gi[a : a + 1])) for a in range(2)]
    blocks = v_ref.shape[1] // LANES
    for block in range(blocks):
        lanes = pl.ds(block * LANES, LANES)
        first = index_rows(index_ref, 0, block, offset)
        second = index_rows(index_ref, 1, block, offset)
        left = [(lookup(re, first), lookup(im, first)) for re, im in sources]
        right = [(lookup(re, second), lookup(im, second)) for re, im in sources]
        for c in range(4):
            (pr, pi), (qr, qi) = left[c // 2], right[c % 2]
            cr, ci = pr * qr + pi * qi, pi * qr - pr * qi
            sr = s_ref[pl.ds(c * 8, 8), lanes]
            si = s_ref[pl.ds(32 + c * 8, 8), lanes]
            mr, mi = cmul(cr, ci, sr, si)
            yield (
                block,
                c,
                v_ref[pl.ds(c * 8, 8), lanes] - mr,
                v_ref[pl.ds(32 + c * 8, 8), lanes] - mi,
            )


def noise_into(v_ref, s_ref, index_ref, gr, gi, power_ref):
    for block, c, rr, ri in residual_blocks(v_ref, s_ref, index_ref, gr, gi):
        term = rr * rr + ri * ri
        total = term if c == 0 else total + term
        if c == 3:
            power_ref[pl.ds(block * 8, 8), :] = total


def fold_rows(ref, count, group):
    whole = group if group % 8 == 0 else math.lcm(group, 8)
    value = jnp.sum(ref[...].reshape(count * group // whole, whole, LANES), axis=0)
    while whole > group and group % 2:
        break
    if whole == group:
        return value
    total = value[0:group]
    for at in range(group, whole, group):
        total = total + value[at : at + group]
    return total


def delay_step(received_ref, delay):
    summed = fold_rows(received_ref, 64, 2)
    step = DAMPING * summed[0:1] / summed[1:2]
    low = low_half((1, LANES))
    turned = half_roll(jnp.broadcast_to(step, (8, LANES)))[0:1]
    both = jnp.concatenate([jnp.where(low, step, turned), jnp.where(low, turned, step)], axis=0)
    return delay + both


def first_kernel(v_ref, s_ref, index_ref, gain_ref, band_ref, delay_ref, x_ref, power_ref):
    _, _, (gr, gi) = chain(gain_ref[...], band_ref[...], delay_ref[...], x_ref[0, 0])
    noise_into(v_ref, s_ref, index_ref, gr, gi, power_ref)


def next_kernel(
    v_ref, s_ref, index_ref, gain_ref, band_ref, delay_ref, received_ref, x_ref, power_ref, new_ref
):
    delay = delay_step(received_ref, delay_ref[...])
    new_ref[...] = delay
    _, _, (gr, gi) = chain(gain_ref[...], band_ref[...], delay, x_ref[0, 0])
    noise_into(v_ref, s_ref, index_ref, gr, gi, power_ref)


def last_kernel(
    v_ref, s_ref, index_ref, gain_ref, band_ref, delay_ref, received_ref, x_ref, out_ref, new_ref
):
    delay = delay_step(received_ref, delay_ref[...])
    new_ref[...] = delay
    _, _, (gr, gi) = chain(gain_ref[...], band_ref[...], delay, x_ref[0, 0])
    for block, c, rr, ri in residual_blocks(v_ref, s_ref, index_ref, gr, gi):
        lanes = pl.ds(block * LANES, LANES)
        out_ref[pl.ds(c * 8, 8), lanes] = rr
        out_ref[pl.ds(32 + c * 8, 8), lanes] = ri


def weight_kernel(scale, parts_ref, out_ref):
    summed = jnp.sum(parts_ref[...].reshape(16, 8, LANES), axis=0)
    summed = summed[0:2] + summed[2:4] + (summed[4:6] + summed[6:8])
    weight = 1.0 / (summed * scale + EPSILON)
    eight = jnp.concatenate([weight] * 4, axis=0)
    for at in range(16):
        out_ref[pl.ds(at * 8, 8), :] = eight


def normal_sums(load_stats, blocks, index_ref, hot_ref, gr, gi, left_ref):
    row = lax.broadcasted_iota(jnp.int32, (8, LANES), 0)
    offset = (row % 2) * HALF
    top = row < 4
    inner = (row // 2) % 2 == 0

    def pick(mask, part):
        return jnp.where(mask, fill(part[0:1]), fill(part[1:2]))

    p_re, p_im = pick(top, gr), pick(top, gi)
    q_re, q_im = pick(inner, gr), pick(inner, gi)
    for block in range(blocks):
        lanes = pl.ds(block * LANES, LANES)
        first = index_rows(index_ref, 0, block, offset)
        second = index_rows(index_ref, 1, block, offset)
        pr, pi = lookup(p_re, first), lookup(p_im, first)
        qr, qi = lookup(q_re, second), lookup(q_im, second)
        cr, ci, power = load_stats(block)
        rr = cr - (pr * qr + pi * qi) * power
        ri = ci - (pi * qr - pr * qi) * power
        terms = jnp.concatenate(
            [
                qr * rr - qi * ri,
                qr * ri + qi * rr,
                (qr * qr + qi * qi) * power,
                pr * rr + pi * ri,
                pi * rr - pr * ri,
                (pr * pr + pi * pi) * power,
            ],
            axis=0,
        )
        high = terms.astype(jnp.bfloat16)
        rest = terms - high.astype(F32)
        middle = rest.astype(jnp.bfloat16)
        low = (rest - middle.astype(F32)).astype(jnp.bfloat16)
        left_ref[0:48, lanes] = high
        left_ref[48:96, lanes] = middle
        left_ref[96:144, lanes] = low
    sums = jnp.dot(left_ref[...], hot_ref[...], preferred_element_type=F32)
    sums = sums[0:48] + (sums[48:96] + sums[96:144])
    turned = half_roll(sums)
    low_lanes = low_half((1, LANES))
    out = []
    for kind in range(3):
        made = []
        for a in range(2):
            p, q = kind * 8 + 4 * a, 24 + kind * 8 + 2 * a

            def at(array, index):
                return array[index : index + 1]

            here = at(sums, p) + at(sums, p + 2) + (at(turned, q) + at(turned, q + 4))
            there = at(turned, p + 1) + at(turned, p + 3) + (at(sums, q + 1) + at(sums, q + 5))
            made.append(jnp.where(low_lanes, here, there))
        out.append(jnp.concatenate(made, axis=0))
    return out


def stats_loader(stats_ref):
    def load(block):
        lanes = pl.ds(block * LANES, LANES)
        return stats_ref[0:8, lanes], stats_ref[8:16, lanes], stats_ref[16:24, lanes]

    return load


def time_kernel(
    v_ref,
    s_ref,
    weight_ref,
    index_ref,
    hot_ref,
    gain_ref,
    band_ref,
    delay_ref,
    x_ref,
    stats_ref,
    send_ref,
    real_ref,
    imag_ref,
    power_ref,
    left_ref,
):
    blocks = v_ref.shape[1] // LANES
    for block in range(blocks):
        lanes = pl.ds(block * LANES, LANES)
        weight = weight_ref[pl.ds(block * 8, 8), :]
        for c in range(4):
            sr, si = s_ref[pl.ds(c * 8, 8), lanes], s_ref[pl.ds(32 + c * 8, 8), lanes]
            vr, vi = v_ref[pl.ds(c * 8, 8), lanes], v_ref[pl.ds(32 + c * 8, 8), lanes]
            xr, xi = conj_mul(sr, si, vr, vi)
            rows = pl.ds(block * 32 + c * 8, 8)
            real_ref[rows, :] = weight * xr
            imag_ref[rows, :] = weight * xi
            power_ref[rows, :] = weight * (sr * sr + si * si)
        for slot, ref in enumerate((real_ref, imag_ref, power_ref)):
            parts = [ref[pl.ds(block * 32 + t, 8, stride=4), :] for t in range(4)]
            stats_ref[slot * 8 : slot * 8 + 8, lanes] = parts[0] + parts[1] + (parts[2] + parts[3])
    _, (hr, hi), (gr, gi) = chain(gain_ref[...], band_ref[...], delay_ref[...], x_ref[0, 0])
    ur, ui, w = normal_sums(stats_loader(stats_ref), blocks, index_ref, hot_ref, gr, gi, left_ref)
    nr, ni = conj_mul(hr, hi, ur, ui)
    packed = jnp.concatenate([nr, ni, (hr * hr + hi * hi) * w], axis=0)
    repeated = jnp.concatenate([packed] * 4, axis=0)
    for at in range(16):
        send_ref[pl.ds(at * 24, 24), :] = repeated


def stepped(numerator_re, numerator_im, denominator):
    return jnp.concatenate(
        [DAMPING * numerator_re / denominator, DAMPING * numerator_im / denominator], axis=0
    )


def band_kernel(
    stats_ref,
    received_ref,
    index_ref,
    hot_ref,
    gain_ref,
    band_ref,
    delay_ref,
    x_ref,
    new_ref,
    send_ref,
    left_ref,
):
    summed = fold_rows(received_ref, 64, 6)
    gain = gain_ref[...] + stepped(summed[0:2], summed[2:4], summed[4:6])
    new_ref[...] = gain
    (kr, ki), _, (gr, gi) = chain(gain, band_ref[...], delay_ref[...], x_ref[0, 0])
    blocks = stats_ref.shape[1] // LANES
    ur, ui, w = normal_sums(stats_loader(stats_ref), blocks, index_ref, hot_ref, gr, gi, left_ref)
    hr, hi = cmul(gain[0:2], gain[2:4], kr, ki)
    nr, ni = conj_mul(hr, hi, ur, ui)
    packed = jnp.concatenate(
        [nr, ni, (hr * hr + hi * hi) * w, jnp.zeros((2, LANES), F32)], axis=0
    )
    send_ref[...] = packed + half_roll(packed)


def delay_kernel(
    stats_ref,
    received_ref,
    index_ref,
    hot_ref,
    gain_ref,
    band_ref,
    delay_ref,
    x_ref,
    new_ref,
    send_ref,
    left_ref,
):
    summed = received_ref[...]
    band = band_ref[...] + stepped(summed[0:2], summed[2:4], summed[4:6])
    new_ref[...] = band
    x = x_ref[0, 0]
    _, _, (gr, gi) = chain(gain_ref[...], band, delay_ref[...], x)
    blocks = stats_ref.shape[1] // LANES
    ur, ui, w = normal_sums(stats_loader(stats_ref), blocks, index_ref, hot_ref, gr, gi, left_ref)
    turning = TURN * x
    n = turning * (gr * ui - gi * ur)
    d = (turning * turning) * ((gr * gr + gi * gi) * w)
    packed = jnp.concatenate([n, d, jnp.zeros((4, LANES), F32)], axis=0)
    packed = packed + half_roll(packed)
    low = low_half((1, LANES))
    pair = jnp.concatenate(
        [jnp.where(low, packed[0:1], packed[1:2]), jnp.where(low, packed[2:3], packed[3:4])],
        axis=0,
    )
    send_ref[...] = jnp.concatenate([pair] * 4, axis=0)


def call(body, outs, operands, scratch=()):
    vmem = pl.BlockSpec(memory_space=pltpu.VMEM)
    smem = pl.BlockSpec(memory_space=pltpu.SMEM)
    return pl.pallas_call(
        body,
        out_shape=tuple(jax.ShapeDtypeStruct(o, F32) for o in outs),
        in_specs=[smem if o.shape == (1, 1) else vmem for o in operands],
        out_specs=tuple(vmem for _ in outs),
        scratch_shapes=list(scratch),
        compiler_params=pltpu.CompilerParams(vmem_limit_bytes=12 << 20),
    )(*operands)


def exchange(array):
    devices = lax.axis_size(FREQ)
    chunks = array.reshape(devices, 1, -1)
    return lax.all_to_all(chunks, FREQ, 0, 0, tiled=True).reshape(array.shape)


def pair_total(array):
    for axis in ("tm_1", "tm_0"):
        array = array + lax.ppermute(array, axis, [(0, 1), (1, 0)])
    return array


def shards(
    visibilities, sky_model, gain_time, gain_band, delay_start, first_antenna, second_antenna
):
    antennas = gain_time.shape[-1]
    baselines = visibilities.shape[4]
    padded = -(-baselines // LANES) * LANES
    times = visibilities.shape[2]
    channels = lax.axis_size(FREQ)
    x = (lax.axis_index(FREQ).astype(F32) + 0.5) / channels - 0.5
    x = x.reshape(1, 1)

    def plane(array):
        flat = array.reshape(-1, baselines)
        return jnp.pad(flat, ((0, 0), (0, padded - baselines)))

    v, s = plane(visibilities), plane(sky_model)
    ids = jnp.stack([first_antenna, second_antenna])
    index = jnp.pad(ids, ((0, 6), (0, padded - baselines)))
    marked = jnp.pad(ids, ((0, 0), (0, padded - baselines)), constant_values=-1)
    hot = jnp.concatenate(
        [marked[k][:, None] == jnp.arange(antennas, dtype=jnp.int32)[None] for k in range(2)],
        axis=1,
    ).astype(jnp.bfloat16)

    gain = gain_time.reshape(4, LANES)
    band = gain_band.reshape(4, antennas)
    band = jnp.concatenate([band, band], axis=1)
    delay = jnp.concatenate([delay_start, delay_start], axis=1)

    left = pltpu.VMEM((144, padded), jnp.bfloat16)
    tall = pltpu.VMEM((padded // LANES * 32, LANES), F32)
    square = (padded // LANES * 8, LANES)
    received = None
    for sweep in range(SWEEPS):
        if sweep == 0:
            (power,) = call(first_kernel, [square], (v, s, index, gain, band, delay, x))
        else:
            power, delay = call(
                next_kernel, [square, delay.shape], (v, s, index, gain, band, delay, received, x)
            )
        (mine,) = call(
            functools.partial(weight_kernel, 1.0 / (4 * channels)), [square], (exchange(power),)
        )
        weight = exchange(mine)
        stats, send = call(
            time_kernel,
            [(24, padded), (384, LANES)],
            (v, s, weight, index, hot, gain, band, delay, x),
            (tall, tall, tall, left),
        )
        gain, send = call(
            band_kernel,
            [gain.shape, (8, LANES)],
            (stats, exchange(send), index, hot, gain, band, delay, x),
            (left,),
        )
        band, send = call(
            delay_kernel,
            [band.shape, (8, LANES)],
            (stats, pair_total(send), index, hot, gain, band, delay, x),
            (left,),
        )
        summed = pair_total(send)
        received = exchange(jnp.broadcast_to(summed[None], (16, 8, LANES)).reshape(128, LANES))
    residual, delay = call(
        last_kernel, [v.shape, delay.shape], (v, s, index, gain, band, delay, received, x)
    )
    weights = weight.reshape(-1, times, LANES).transpose(1, 0, 2).reshape(times, padded)
    return (
        gain.reshape(gain_time.shape),
        band[:, :antennas].reshape(gain_band.shape),
        delay[:, :antennas],
        weights[:, :baselines],
        residual[:, :baselines].reshape(visibilities.shape),
    )


def solution(mesh):
    split = Mesh(
        mesh.devices.reshape(2, 2, 4, 2, 8), ("tm_0", "tm_1", "freq_0", "freq_1", "freq_2")
    )
    placed = (
        P(None, None, TM, FREQ, None),
        P(None, None, TM, FREQ, None),
        P(None, None, TM, None),
        P(None, None, FREQ, None),
        P(),
        P(),
        P(),
    )
    return jax.shard_map(
        shards,
        mesh=split,
        in_specs=placed,
        out_specs=(
            P(None, None, TM, None),
            P(None, None, FREQ, None),
            P(),
            P(TM, None),
            P(None, None, TM, FREQ, None),
        ),
        check_vma=False,
    )
```

```python
import functools
import math

import jax
import jax.numpy as jnp
from jax import lax
from jax.experimental import pallas as pl
from jax.experimental.pallas import tpu as pltpu
from jax.sharding import Mesh
from jax.sharding import PartitionSpec as P

SWEEPS = 2
TURN = 2.0 * math.pi
DAMPING = 0.5
EPSILON = 1e-06
LANES = 128
HALF = 64
FREQ = ("freq_0", "freq_1", "freq_2")
TM = ("tm_0", "tm_1")
YX = ("freq_0", "freq_1")
Z = "freq_2"
F32 = jnp.float32


def half_roll(array):
    return pltpu.roll(array, HALF, 1)


def low_half(shape):
    return lax.broadcasted_iota(jnp.int32, shape, 1) < HALF


def cmul(ar, ai, br, bi):
    return ar * br - ai * bi, ar * bi + ai * br


def conj_mul(ar, ai, br, bi):
    return ar * br + ai * bi, ar * bi - ai * br


def chain(gain, band, delay, x):
    angle = TURN * delay * x
    kr, ki = jnp.cos(angle), jnp.sin(angle)
    hr, hi = cmul(band[0:2], band[2:4], kr, ki)
    gr, gi = cmul(gain[0:2], gain[2:4], hr, hi)
    return (kr, ki), (hr, hi), (gr, gi)


def fill(row):
    return jnp.broadcast_to(row, (8, LANES))


def index_rows(index_ref, side, block, offset):
    row = index_ref[side : side + 1, block * LANES : (block + 1) * LANES]
    return fill(row) + offset


def lookup(source, index):
    return jnp.take_along_axis(source, index, axis=1)


def residual_blocks(v_ref, s_ref, index_ref, gr, gi):
    offset = jnp.where(lax.broadcasted_iota(jnp.int32, (8, LANES), 0) >= 4, HALF, 0)
    sources = [(fill(gr[a : a + 1]), fill(gi[a : a + 1])) for a in range(2)]
    blocks = v_ref.shape[1] // LANES
    for block in range(blocks):
        lanes = pl.ds(block * LANES, LANES)
        first = index_rows(index_ref, 0, block, offset)
        second = index_rows(index_ref, 1, block, offset)
        left = [(lookup(re, first), lookup(im, first)) for re, im in sources]
        right = [(lookup(re, second), lookup(im, second)) for re, im in sources]
        for c in range(4):
            (pr, pi), (qr, qi) = left[c // 2], right[c % 2]
            cr, ci = pr * qr + pi * qi, pi * qr - pr * qi
            sr = s_ref[pl.ds(c * 8, 8), lanes]
            si = s_ref[pl.ds(32 + c * 8, 8), lanes]
            mr, mi = cmul(cr, ci, sr, si)
            yield (
                block,
                c,
                v_ref[pl.ds(c * 8, 8), lanes] - mr,
                v_ref[pl.ds(32 + c * 8, 8), lanes] - mi,
            )


def noise_into(v_ref, s_ref, index_ref, gr, gi, power_ref):
    for block, c, rr, ri in residual_blocks(v_ref, s_ref, index_ref, gr, gi):
        term = rr * rr + ri * ri
        total = term if c == 0 else total + term
        if c == 3:
            power_ref[pl.ds(block * 8, 8), :] = total


def fold_rows(ref, count, group):
    whole = group if group % 8 == 0 else math.lcm(group, 8)
    value = jnp.sum(ref[...].reshape(count * group // whole, whole, LANES), axis=0)
    if whole == group:
        return value
    total = value[0:group]
    for at in range(group, whole, group):
        total = total + value[at : at + group]
    return total


def delay_step(received_ref, delay):
    summed = fold_rows(received_ref, 64, 2)
    step = DAMPING * summed[0:1] / summed[1:2]
    low = low_half((1, LANES))
    turned = half_roll(jnp.broadcast_to(step, (8, LANES)))[0:1]
    both = jnp.concatenate([jnp.where(low, step, turned), jnp.where(low, turned, step)], axis=0)
    return delay + both


def side_by_side(left, right):
    return jnp.concatenate([left, right], axis=1)


def first_kernel(
    v_ref,
    s_ref,
    first_ref,
    second_ref,
    time_ref,
    channel_ref,
    start_ref,
    x_ref,
    power_ref,
    gain_ref,
    band_ref,
    delay_ref,
    index_ref,
    hot_ref,
):
    parts = [(part, a) for part in range(2) for a in range(2)]
    gain = jnp.concatenate(
        [side_by_side(time_ref[p, a, 0:1], time_ref[p, a, 1:2]) for p, a in parts], axis=0
    )
    band = jnp.concatenate([channel_ref[p, a] for p, a in parts], axis=0)
    band = side_by_side(band, band)
    delay = side_by_side(start_ref[...], start_ref[...])
    gain_ref[...] = gain
    band_ref[...] = band
    delay_ref[...] = delay
    baselines = first_ref.shape[1]
    padded = index_ref.shape[1]
    blocks = padded // LANES
    for block in range(blocks):
        at, end = block * LANES, min((block + 1) * LANES, baselines)
        for side, ref in enumerate((first_ref, second_ref)):
            row = ref[0:1, at:end]
            if end < at + LANES:
                row = side_by_side(row, jnp.zeros((1, at + LANES - end), jnp.int32))
            index_ref[side : side + 1, pl.ds(at, LANES)] = row
    number = lax.broadcasted_iota(jnp.int32, (HALF, LANES), 0)
    pairs = blocks // 2
    for block in range(blocks):
        at, half = block % pairs, block // pairs
        for side in range(2):
            row = index_ref[side : side + 1, pl.ds(block * LANES, LANES)]
            same = jnp.broadcast_to(row, (HALF, LANES)) == number
            rows = pl.ds((half * 2 + side) * HALF, HALF)
            hot_ref[rows, pl.ds(at * LANES, LANES)] = jnp.where(same, 1.0, 0.0).astype(
                jnp.bfloat16
            )
    _, _, (gr, gi) = chain(gain, band, delay, x_ref[0, 0])
    noise_into(v_ref, s_ref, index_ref, gr, gi, power_ref)


def next_kernel(
    v_ref, s_ref, index_ref, gain_ref, band_ref, delay_ref, received_ref, x_ref, power_ref, new_ref
):
    delay = delay_step(received_ref, delay_ref[...])
    new_ref[...] = delay
    _, _, (gr, gi) = chain(gain_ref[...], band_ref[...], delay, x_ref[0, 0])
    noise_into(v_ref, s_ref, index_ref, gr, gi, power_ref)


def last_kernel(
    v_ref, s_ref, index_ref, gain_ref, band_ref, delay_ref, received_ref, x_ref, out_ref, new_ref
):
    delay = delay_step(received_ref, delay_ref[...])
    new_ref[...] = delay
    _, _, (gr, gi) = chain(gain_ref[...], band_ref[...], delay, x_ref[0, 0])
    for block, c, rr, ri in residual_blocks(v_ref, s_ref, index_ref, gr, gi):
        lanes = pl.ds(block * LANES, LANES)
        out_ref[pl.ds(c * 8, 8), lanes] = rr
        out_ref[pl.ds(32 + c * 8, 8), lanes] = ri


def copies(value, out_ref):
    rows = value.shape[0]
    for at in range(0, out_ref.shape[0], rows):
        out_ref[pl.ds(at, rows), :] = value


def spread_kernel(parts_ref, out_ref):
    copies(jnp.sum(parts_ref[...].reshape(8, 16, LANES), axis=0), out_ref)


def weight_kernel(scale, parts_ref, out_ref):
    summed = jnp.sum(parts_ref[...].reshape(8, 16, LANES), axis=0)
    copies(1.0 / (summed * scale + EPSILON), out_ref)


def split_into(left_ref, lanes, terms):
    high = terms.astype(jnp.bfloat16)
    rest = terms - high.astype(F32)
    middle = rest.astype(jnp.bfloat16)
    low = (rest - middle.astype(F32)).astype(jnp.bfloat16)
    left_ref[0:48, lanes] = high
    left_ref[48:96, lanes] = middle
    left_ref[96:144, lanes] = low


def joined(sums):
    return sums[0:48] + (sums[48:96] + sums[96:144])


def contract(left, right):
    return lax.dot_general(left, right, (((1,), (1,)), ((), ())), preferred_element_type=F32)


def terms_of(pr, pi, qr, qi, cr, ci, power):
    rr = cr - (pr * qr + pi * qi) * power
    ri = ci - (pi * qr - pr * qi) * power
    return jnp.concatenate(
        [
            qr * rr - qi * ri,
            qr * ri + qi * rr,
            (qr * qr + qi * qi) * power,
            pr * rr + pi * ri,
            pi * rr - pr * ri,
            (pr * pr + pi * pi) * power,
        ],
        axis=0,
    )


def packed_sources(gr, gi):
    row = lax.broadcasted_iota(jnp.int32, (8, LANES), 0)
    offset = (row % 2) * HALF
    top = row < 4
    inner = (row // 2) % 2 == 0

    def pick(mask, part):
        return jnp.where(mask, fill(part[0:1]), fill(part[1:2]))

    return pick(top, gr), pick(top, gi), pick(inner, gr), pick(inner, gi), offset


def packed_lookup(sources, index_ref, block):
    p_re, p_im, q_re, q_im, offset = sources
    first = index_rows(index_ref, 0, block, offset)
    second = index_rows(index_ref, 1, block, offset)
    return lookup(p_re, first), lookup(p_im, first), lookup(q_re, second), lookup(q_im, second)


def interval_sums(stats_ref, index_ref, hot_ref, gr, gi, left_ref):
    sources = packed_sources(gr, gi)
    padded = stats_ref.shape[1]
    for block in range(padded // LANES):
        lanes = pl.ds(block * LANES, LANES)
        stats = stats_ref[0:8, lanes], stats_ref[8:16, lanes], stats_ref[16:24, lanes]
        split_into(left_ref, lanes, terms_of(*packed_lookup(sources, index_ref, block), *stats))
    middle = padded // 2
    sums = contract(left_ref[:, 0:middle], hot_ref[0:LANES, :]) + contract(
        left_ref[:, middle:padded], hot_ref[LANES : 2 * LANES, :]
    )
    sums = joined(sums)
    turned = half_roll(sums)
    low_lanes = low_half((1, LANES))
    out = []
    for kind in range(3):
        made = []
        for a in range(2):
            p, q = kind * 8 + 4 * a, 24 + kind * 8 + 2 * a

            def at(array, index):
                return array[index : index + 1]

            here = at(sums, p) + at(sums, p + 2) + (at(turned, q) + at(turned, q + 4))
            there = at(turned, p + 1) + at(turned, p + 3) + (at(sums, q + 1) + at(sums, q + 5))
            made.append(jnp.where(low_lanes, here, there))
        out.append(jnp.concatenate(made, axis=0))
    return out


def paired_sums(mix_ref, index_ref, hot_ref, hr, hi, left_ref):
    row = lax.broadcasted_iota(jnp.int32, (8, LANES), 0)
    top = row < 4
    alpha, beta = (row // 2) % 2 == 0, row % 2 == 0

    def pick(mask, part):
        return jnp.where(mask, fill(part[0:1]), fill(part[1:2]))

    p_re, p_im, q_re, q_im = pick(alpha, hr), pick(alpha, hi), pick(beta, hr), pick(beta, hi)
    pairs = mix_ref.shape[1] // LANES
    for block in range(pairs):
        lanes = pl.ds(block * LANES, LANES)
        first, second = (
            jnp.where(
                top,
                index_rows(index_ref, side, block, 0),
                index_rows(index_ref, side, block + pairs, 0),
            )
            for side in range(2)
        )
        stats = mix_ref[0:8, lanes], mix_ref[8:16, lanes], mix_ref[16:24, lanes]
        terms = terms_of(
            lookup(p_re, first),
            lookup(p_im, first),
            lookup(q_re, second),
            lookup(q_im, second),
            *stats,
        )
        split_into(left_ref, lanes, terms)
    sums = joined(contract(left_ref[...], hot_ref[...]))
    out = []
    low = low_half((2, LANES))
    for kind in range(3):

        def rows(start):
            return sums[start : start + 4, 0:LANES] + sums[start + 4 : start + 8, LANES:]

        p, q = rows(kind * 8), rows(24 + kind * 8)
        p = jnp.concatenate([p[0:1] + p[1:2], p[2:3] + p[3:4]], axis=0)
        q = q[0:2] + q[2:4]
        value = p + half_roll(q)
        out.append(jnp.where(low, value, half_roll(value)))
    return out


def time_kernel(
    v_ref,
    s_ref,
    weight_ref,
    index_ref,
    hot_ref,
    gain_ref,
    band_ref,
    delay_ref,
    x_ref,
    stats_ref,
    send_ref,
    kept_ref,
    real_ref,
    imag_ref,
    power_ref,
    left_ref,
):
    blocks = v_ref.shape[1] // LANES
    baselines = kept_ref.shape[1]
    for block in range(blocks):
        lanes = pl.ds(block * LANES, LANES)
        weight = weight_ref[pl.ds(block * 8, 8), :]
        width = min(LANES, baselines - block * LANES)
        kept_ref[:, pl.ds(block * LANES, width)] = weight[:, 0:width]
        for c in range(4):
            sr, si = s_ref[pl.ds(c * 8, 8), lanes], s_ref[pl.ds(32 + c * 8, 8), lanes]
            vr, vi = v_ref[pl.ds(c * 8, 8), lanes], v_ref[pl.ds(32 + c * 8, 8), lanes]
            xr, xi = conj_mul(sr, si, vr, vi)
            rows = pl.ds(block * 32 + c * 8, 8)
            real_ref[rows, :] = weight * xr
            imag_ref[rows, :] = weight * xi
            power_ref[rows, :] = weight * (sr * sr + si * si)
        for slot, ref in enumerate((real_ref, imag_ref, power_ref)):
            parts = [ref[pl.ds(block * 32 + t, 8, stride=4), :] for t in range(4)]
            stats_ref[slot * 8 : slot * 8 + 8, lanes] = parts[0] + parts[1] + (parts[2] + parts[3])
    _, (hr, hi), (gr, gi) = chain(gain_ref[...], band_ref[...], delay_ref[...], x_ref[0, 0])
    ur, ui, w = interval_sums(stats_ref, index_ref, hot_ref, gr, gi, left_ref)
    nr, ni = conj_mul(hr, hi, ur, ui)
    packed = jnp.concatenate([nr, ni, (hr * hr + hi * hi) * w], axis=0)
    repeated = jnp.concatenate([packed] * 4, axis=0)
    for at in range(16):
        send_ref[pl.ds(at * 24, 24), :] = repeated


def stepped(numerator_re, numerator_im, denominator):
    return jnp.concatenate(
        [DAMPING * numerator_re / denominator, DAMPING * numerator_im / denominator], axis=0
    )


def mix_kernel(
    stats_ref, received_ref, index_ref, gain_ref, new_ref, mix_ref, real_ref, imag_ref, power_ref
):
    summed = fold_rows(received_ref, 64, 6)
    gain = gain_ref[...] + stepped(summed[0:2], summed[2:4], summed[4:6])
    new_ref[...] = gain
    sources = packed_sources(gain[0:2], gain[2:4])
    blocks = stats_ref.shape[1] // LANES
    pairs = blocks // 2
    for block in range(blocks):
        lanes = pl.ds(block * LANES, LANES)
        pr, pi, qr, qi = packed_lookup(sources, index_ref, block)
        er, ei = conj_mul(pr, pi, qr, qi)
        ar, ai = cmul(er, ei, stats_ref[0:8, lanes], stats_ref[8:16, lanes])
        rows = pl.ds((block % pairs) * 16 + (block // pairs) * 8, 8)
        real_ref[rows, :] = ar
        imag_ref[rows, :] = ai
        power_ref[rows, :] = (pr * pr + pi * pi) * ((qr * qr + qi * qi) * stats_ref[16:24, lanes])
    for pair in range(pairs):
        lanes = pl.ds(pair * LANES, LANES)
        for slot, ref in enumerate((real_ref, imag_ref, power_ref)):
            mix_ref[slot * 8 : slot * 8 + 8, lanes] = (
                ref[pl.ds(pair * 16, 8, stride=2), :] + ref[pl.ds(pair * 16 + 1, 8, stride=2), :]
            )


def solve_kernel(
    mix_ref, index_ref, hot_ref, band_ref, delay_ref, x_ref, new_ref, send_ref, left_ref
):
    x = x_ref[0, 0]
    angle = TURN * delay_ref[...] * x
    kr, ki = jnp.cos(angle), jnp.sin(angle)
    band = band_ref[...]
    hr, hi = cmul(band[0:2], band[2:4], kr, ki)
    ur, ui, w = paired_sums(mix_ref, index_ref, hot_ref, hr, hi, left_ref)
    nr, ni = conj_mul(kr, ki, ur, ui)
    band = band + stepped(nr, ni, (kr * kr + ki * ki) * w)
    new_ref[...] = band
    hr, hi = cmul(band[0:2], band[2:4], kr, ki)
    ur, ui, w = paired_sums(mix_ref, index_ref, hot_ref, hr, hi, left_ref)
    turning = TURN * x
    n = turning * (hr * ui - hi * ur)
    d = (turning * turning) * ((hr * hr + hi * hi) * w)
    low = low_half((1, LANES))
    pair = jnp.concatenate(
        [jnp.where(low, n[0:1], n[1:2]), jnp.where(low, d[0:1], d[1:2])], axis=0
    )
    copies(jnp.concatenate([pair] * 4, axis=0), send_ref)


def call(body, outs, operands, scratch=()):
    vmem = pl.BlockSpec(memory_space=pltpu.VMEM)
    smem = pl.BlockSpec(memory_space=pltpu.SMEM)
    return pl.pallas_call(
        body,
        out_shape=tuple(
            o if isinstance(o, jax.ShapeDtypeStruct) else jax.ShapeDtypeStruct(o, F32)
            for o in outs
        ),
        in_specs=[smem if o.shape == (1, 1) else vmem for o in operands],
        out_specs=tuple(vmem for _ in outs),
        scratch_shapes=list(scratch),
        compiler_params=pltpu.CompilerParams(vmem_limit_bytes=12 << 20),
    )(*operands)


def exchange(array, axis):
    devices = lax.axis_size(axis)
    chunks = array.reshape(devices, 1, -1)
    return lax.all_to_all(chunks, axis, 0, 0, tiled=True).reshape(array.shape)


def pair_total(array):
    for axis in ("tm_1", "tm_0"):
        array = array + lax.ppermute(array, axis, [(0, 1), (1, 0)])
    return array


def shards(
    visibilities, sky_model, gain_time, gain_band, delay_start, first_antenna, second_antenna
):
    antennas = gain_time.shape[-1]
    baselines = visibilities.shape[4]
    padded = -(-baselines // (2 * LANES)) * 2 * LANES
    blocks = padded // LANES
    times = visibilities.shape[2]
    channels = lax.axis_size(FREQ)
    x = (lax.axis_index(FREQ).astype(F32) + 0.5) / channels - 0.5
    x = x.reshape(1, 1)

    def plane(array):
        flat = array.reshape(-1, baselines)
        return jnp.pad(flat, ((0, 0), (0, padded - baselines)))

    v, s = plane(visibilities), plane(sky_model)
    square = (blocks * 8, LANES)
    left = pltpu.VMEM((144, padded), jnp.bfloat16)
    half_left = pltpu.VMEM((144, padded // 2), jnp.bfloat16)
    tall = pltpu.VMEM((blocks * 32, LANES), F32)
    short = pltpu.VMEM(square, F32)
    power, gain, band, delay, index, hot = call(
        first_kernel,
        [
            square,
            (4, LANES),
            (4, LANES),
            (2, LANES),
            jax.ShapeDtypeStruct((8, padded), jnp.int32),
            jax.ShapeDtypeStruct((4 * HALF, padded // 2), jnp.bfloat16),
        ],
        (
            v,
            s,
            first_antenna.reshape(1, -1),
            second_antenna.reshape(1, -1),
            gain_time,
            gain_band,
            delay_start,
            x,
        ),
    )
    for sweep in range(SWEEPS):
        if sweep > 0:
            power, delay = call(
                next_kernel, [square, delay.shape], (v, s, index, gain, band, delay, received, x)
            )
        (shared,) = call(spread_kernel, [square], (exchange(power, Z),))
        (mine,) = call(
            functools.partial(weight_kernel, 1.0 / (4 * channels)),
            [square],
            (exchange(shared, YX),),
        )
        weight = exchange(mine, Z)
        outs, scratch = [(24, padded), (384, LANES)], [tall, tall, tall, left]
        if sweep < SWEEPS - 1:
            scratch = [pltpu.VMEM((times, baselines), F32)] + scratch
        else:
            outs = outs + [(times, baselines)]
        stats, send, *kept = call(
            time_kernel, outs, (v, s, weight, index, hot, gain, band, delay, x), scratch
        )
        gain, mix = call(
            mix_kernel,
            [gain.shape, (24, padded // 2)],
            (stats, exchange(send, FREQ), index, gain),
            (short, short, short),
        )
        band, send = call(
            solve_kernel,
            [band.shape, (128, LANES)],
            (pair_total(mix), index, hot, band, delay, x),
            (half_left,),
        )
        received = exchange(send, FREQ)
    residual, delay = call(
        last_kernel, [v.shape, delay.shape], (v, s, index, gain, band, delay, received, x)
    )
    return (
        gain.reshape(gain_time.shape),
        band[:, :antennas].reshape(gain_band.shape),
        delay[:, :antennas],
        kept[0],
        residual[:, :baselines].reshape(visibilities.shape),
    )


def solution(mesh):
    split = Mesh(
        mesh.devices.reshape(2, 2, 4, 2, 8), ("tm_0", "tm_1", "freq_0", "freq_1", "freq_2")
    )
    placed = (
        P(None, None, TM, FREQ, None),
        P(None, None, TM, FREQ, None),
        P(None, None, TM, None),
        P(None, None, FREQ, None),
        P(),
        P(),
        P(),
    )
    return jax.shard_map(
        shards,
        mesh=split,
        in_specs=placed,
        out_specs=(
            P(None, None, TM, None),
            P(None, None, FREQ, None),
            P(),
            P(TM, None),
            P(None, None, TM, FREQ, None),
        ),
        check_vma=False,
    )
```

```python
import functools
import math

import jax
import jax.numpy as jnp
from jax import lax
from jax.experimental import pallas as pl
from jax.experimental.pallas import tpu as pltpu
from jax.sharding import Mesh
from jax.sharding import PartitionSpec as P

SWEEPS = 2
TURN = 2.0 * math.pi
DAMPING = 0.5
EPSILON = 1e-06
LANES = 128
HALF = 64
PLANES = 64
CHUNK = 4 * PLANES + 8
FREQ = ("freq_0", "freq_1", "freq_2")
TM = ("tm_0", "tm_1")
YX = ("freq_0", "freq_1")
Z = "freq_2"
F32 = jnp.float32


def half_roll(array):
    return pltpu.roll(array, HALF, 1)


def low_half(shape):
    return lax.broadcasted_iota(jnp.int32, shape, 1) < HALF


def cmul(ar, ai, br, bi):
    return ar * br - ai * bi, ar * bi + ai * br


def conj_mul(ar, ai, br, bi):
    return ar * br + ai * bi, ar * bi - ai * br


def chain(gain, band, delay, x):
    angle = TURN * delay * x
    kr, ki = jnp.cos(angle), jnp.sin(angle)
    hr, hi = cmul(band[0:2], band[2:4], kr, ki)
    gr, gi = cmul(gain[0:2], gain[2:4], hr, hi)
    return (kr, ki), (hr, hi), (gr, gi)


def fill(row):
    return jnp.broadcast_to(row, (8, LANES))


def index_rows(index_ref, side, block, offset):
    return fill(index_ref[block * 8 + side : block * 8 + side + 1, :]) + offset


def lookup(source, index):
    return jnp.take_along_axis(source, index, axis=1)


def cell_base(chunk, inner):
    return chunk * CHUNK + inner * PLANES


def parts_of(data_ref, base, c):
    return tuple(
        data_ref[pl.ds(base + kind * 2 * PLANES + part * 32 + c * 8, 8), :]
        for kind in range(2)
        for part in range(2)
    )


def residual_of(data_ref, base, left, right):
    for c in range(4):
        (pr, pi), (qr, qi) = left[c // 2], right[c % 2]
        cr, ci = pr * qr + pi * qi, pi * qr - pr * qi
        vr, vi, sr, si = parts_of(data_ref, base, c)
        mr, mi = cmul(cr, ci, sr, si)
        yield c, vr - mr, vi - mi


def time_offset():
    return jnp.where(lax.broadcasted_iota(jnp.int32, (8, LANES), 0) >= 4, HALF, 0)


def stacked(pair):
    return jnp.concatenate([fill(pair[0:1]), fill(pair[1:2])], axis=0)


def band_chain(bands, delay, x0, step):
    row = lax.broadcasted_iota(jnp.int32, (16, LANES), 0) % 8
    x = x0 + step * row.astype(F32)
    angle = TURN * stacked(delay) * x
    return cmul(bands[0:16], bands[16:32], jnp.cos(angle), jnp.sin(angle))


def noise_into(data_ref, mine_ref, gain, bands, delay, x0, step, power_ref):
    hr, hi = band_chain(bands, delay, x0, step)
    gr, gi = cmul(stacked(gain[0:2]), stacked(gain[2:4]), hr, hi)
    offset = time_offset()
    index = [[index_rows(mine_ref, side, inner, offset) for side in range(2)] for inner in range(2)]
    totals = [None, None]
    for k in range(8):
        sources = [
            (fill(gr[a * 8 + k : a * 8 + k + 1]), fill(gi[a * 8 + k : a * 8 + k + 1]))
            for a in range(2)
        ]
        for inner in range(2):
            left, right = (
                [(lookup(re, at), lookup(im, at)) for re, im in sources] for at in index[inner]
            )
            for _, rr, ri in residual_of(data_ref, cell_base(k, inner), left, right):
                term = rr * rr + ri * ri
                totals[inner] = term if totals[inner] is None else totals[inner] + term
    copies(jnp.concatenate(totals, axis=0), power_ref)


def delay_step(received_ref, delay):
    summed = jnp.sum(received_ref[...].reshape(32, 8, LANES), axis=0)
    summed = summed[0:4] + summed[4:8]
    step = DAMPING * summed[0:1] / summed[1:2]
    low = low_half((1, LANES))
    turned = half_roll(jnp.broadcast_to(step, (8, LANES)))[0:1]
    both = jnp.concatenate([jnp.where(low, step, turned), jnp.where(low, turned, step)], axis=0)
    return delay + both


def side_by_side(left, right):
    return jnp.concatenate([left, right], axis=1)


def arrange_kernel(v_ref, s_ref, channel_ref, data_ref):
    baselines = v_ref.shape[1]
    band = own_band(channel_ref)
    for chunk in range(8):
        for inner in range(2):
            at = (2 * chunk + inner) * LANES
            end = min(at + LANES, baselines)
            for kind, ref in enumerate((v_ref, s_ref)):
                value = ref[:, at:end]
                if end < at + LANES:
                    value = side_by_side(value, jnp.zeros((PLANES, at + LANES - end), F32))
                data_ref[pl.ds(cell_base(chunk, inner) + kind * 2 * PLANES, PLANES), :] = value
        data_ref[pl.ds(chunk * CHUNK + 4 * PLANES, 8), :] = jnp.concatenate([band, band], axis=0)


def own_band(channel_ref):
    parts = [(part, a) for part in range(2) for a in range(2)]
    band = jnp.concatenate([channel_ref[p, a] for p, a in parts], axis=0)
    return side_by_side(band, band)


def table_kernel(
    first_ref,
    second_ref,
    time_ref,
    channel_ref,
    start_ref,
    member_ref,
    gain_ref,
    band_ref,
    delay_ref,
    index_ref,
    hot_ref,
    mine_ref,
    mine_hot_ref,
):
    parts = [(part, a) for part in range(2) for a in range(2)]
    gain_ref[...] = jnp.concatenate(
        [side_by_side(time_ref[p, a, 0:1], time_ref[p, a, 1:2]) for p, a in parts], axis=0
    )
    band_ref[...] = own_band(channel_ref)
    delay_ref[...] = side_by_side(start_ref[...], start_ref[...])
    baselines = first_ref.shape[1]
    blocks = index_ref.shape[0] // 8
    for block in range(blocks):
        at, end = block * LANES, min((block + 1) * LANES, baselines)
        rows = []
        for ref in (first_ref, second_ref):
            row = ref[0:1, at:end]
            if end < at + LANES:
                row = side_by_side(row, jnp.zeros((1, at + LANES - end), jnp.int32))
            rows.append(row)
        index_ref[pl.ds(block * 8, 8), :] = jnp.concatenate(rows * 4, axis=0)
    number = lax.broadcasted_iota(jnp.int32, (HALF, LANES), 0)

    def marks(ref, block, side):
        row = ref[block * 8 + side : block * 8 + side + 1, :]
        same = jnp.broadcast_to(row, (HALF, LANES)) == number
        return jnp.where(same, 1.0, 0.0).astype(jnp.bfloat16)

    pairs = blocks // 2
    for block in range(blocks):
        at, half = block % pairs, block // pairs
        for side in range(2):
            rows = pl.ds((half * 2 + side) * HALF, HALF)
            hot_ref[rows, pl.ds(at * LANES, LANES)] = marks(index_ref, block, side)
    mine_ref[...] = index_ref[pl.ds(pl.multiple_of(member_ref[0, 0] * 16, 16), 16), :]
    for inner in range(2):
        for side in range(2):
            mine_hot_ref[pl.ds(side * HALF, HALF), pl.ds(inner * LANES, LANES)] = marks(
                mine_ref, inner, side
            )


def first_kernel(
    step, data_ref, mine_ref, gain_ref, delay_ref, x_ref, power_ref, bands_ref
):
    at = [k * CHUNK + 4 * PLANES for k in range(8)]
    bands = jnp.concatenate(
        [data_ref[at[k] + r : at[k] + r + 1, :] for r in range(4) for k in range(8)], axis=0
    )
    bands_ref[...] = bands
    noise_into(
        data_ref, mine_ref, gain_ref[...], bands, delay_ref[...], x_ref[0, 0], step, power_ref
    )


def next_kernel(
    step,
    data_ref,
    mine_ref,
    gain_ref,
    delay_ref,
    received_ref,
    z_ref,
    x_ref,
    power_ref,
    bands_ref,
    new_ref,
):
    delay = delay_step(received_ref, delay_ref[...])
    new_ref[...] = delay
    z = z_ref[0, 0]
    re, im = [], []
    odd = z % 2 == 1
    for k in range(8):
        value = jnp.zeros((8, LANES), F32)
        for j in range(4):
            found = received_ref[pl.ds(k * 32 + j * 8, 8), :]
            value = jnp.where(z // 2 == j, found, value)
        value = jnp.where(odd, value[4:8], value[0:4])
        re.append(value[2:3])
        im.append(value[3:4])
    low = low_half((8, LANES))
    bands = []
    for rows in (re, im):
        value = jnp.concatenate(rows, axis=0)
        turned = half_roll(value)
        bands += [jnp.where(low, value, turned), jnp.where(low, turned, value)]
    bands = jnp.concatenate(bands, axis=0)
    bands_ref[...] = bands
    noise_into(data_ref, mine_ref, gain_ref[...], bands, delay, x_ref[0, 0], step, power_ref)


def last_kernel(
    data_ref, index_ref, gain_ref, band_ref, delay_ref, received_ref, x_ref, out_ref, new_ref
):
    delay = delay_step(received_ref, delay_ref[...])
    new_ref[...] = delay
    _, _, (gr, gi) = chain(gain_ref[...], band_ref[...], delay, x_ref[0, 0])
    offset = time_offset()
    sources = [(fill(gr[a : a + 1]), fill(gi[a : a + 1])) for a in range(2)]
    for block in range(index_ref.shape[0] // 8):
        left, right = (
            [(lookup(re, at), lookup(im, at)) for re, im in sources]
            for at in (index_rows(index_ref, side, block, offset) for side in range(2))
        )
        lanes = pl.ds(block * LANES, LANES)
        base = cell_base(block // 2, block % 2)
        for c, rr, ri in residual_of(data_ref, base, left, right):
            out_ref[pl.ds(c * 8, 8), lanes] = rr
            out_ref[pl.ds(32 + c * 8, 8), lanes] = ri


def copies(value, out_ref):
    rows = value.shape[0]
    for at in range(0, out_ref.shape[0], rows):
        out_ref[pl.ds(at, rows), :] = value


def split_into(left_ref, lanes, terms):
    high = terms.astype(jnp.bfloat16)
    rest = terms - high.astype(F32)
    middle = rest.astype(jnp.bfloat16)
    low = (rest - middle.astype(F32)).astype(jnp.bfloat16)
    left_ref[0:48, lanes] = high
    left_ref[48:96, lanes] = middle
    left_ref[96:144, lanes] = low


def joined(sums):
    return sums[0:48] + (sums[48:96] + sums[96:144])


def contract(left, right):
    return lax.dot_general(left, right, (((1,), (1,)), ((), ())), preferred_element_type=F32)


def terms_of(pr, pi, qr, qi, cr, ci, power):
    rr = cr - (pr * qr + pi * qi) * power
    ri = ci - (pi * qr - pr * qi) * power
    return jnp.concatenate(
        [
            qr * rr - qi * ri,
            qr * ri + qi * rr,
            (qr * qr + qi * qi) * power,
            pr * rr + pi * ri,
            pi * rr - pr * ri,
            (pr * pr + pi * pi) * power,
        ],
        axis=0,
    )


def packed_sources(gr, gi):
    row = lax.broadcasted_iota(jnp.int32, (8, LANES), 0)
    offset = (row % 2) * HALF
    top = row < 4
    inner = (row // 2) % 2 == 0

    def pick(mask, part):
        return jnp.where(mask, fill(part[0:1]), fill(part[1:2]))

    return pick(top, gr), pick(top, gi), pick(inner, gr), pick(inner, gi), offset


def packed_lookup(sources, index_ref, block):
    p_re, p_im, q_re, q_im, offset = sources
    first = index_rows(index_ref, 0, block, offset)
    second = index_rows(index_ref, 1, block, offset)
    return lookup(p_re, first), lookup(p_im, first), lookup(q_re, second), lookup(q_im, second)


def packed_stats(data_ref, base, weight, scratch):
    for c in range(4):
        vr, vi, sr, si = parts_of(data_ref, base, c)
        xr, xi = conj_mul(sr, si, vr, vi)
        for ref, value in zip(scratch, (xr, xi, sr * sr + si * si)):
            ref[pl.ds(c * 8, 8), :] = weight * value
    out = []
    for ref in scratch:
        parts = [ref[pl.ds(t, 8, stride=4), :] for t in range(4)]
        out.append(parts[0] + parts[1] + (parts[2] + parts[3]))
    return out


def antenna_rows(sums):
    turned = half_roll(sums)
    low_lanes = low_half((1, LANES))
    out = []
    for kind in range(3):
        made = []
        for a in range(2):
            p, q = kind * 8 + 4 * a, 24 + kind * 8 + 2 * a

            def at(array, index):
                return array[index : index + 1]

            here = at(sums, p) + at(sums, p + 2) + (at(turned, q) + at(turned, q + 4))
            there = at(turned, p + 1) + at(turned, p + 3) + (at(sums, q + 1) + at(sums, q + 5))
            made.append(jnp.where(low_lanes, here, there))
        out.append(jnp.concatenate(made, axis=0))
    return out


def paired_sums(mix_ref, index_ref, hot_ref, hr, hi, left_ref):
    row = lax.broadcasted_iota(jnp.int32, (8, LANES), 0)
    top = row < 4
    alpha, beta = (row // 2) % 2 == 0, row % 2 == 0

    def pick(mask, part):
        return jnp.where(mask, fill(part[0:1]), fill(part[1:2]))

    p_re, p_im, q_re, q_im = pick(alpha, hr), pick(alpha, hi), pick(beta, hr), pick(beta, hi)
    pairs = mix_ref.shape[1] // LANES
    for block in range(pairs):
        lanes = pl.ds(block * LANES, LANES)
        first, second = (
            jnp.where(
                top,
                index_rows(index_ref, side, block, 0),
                index_rows(index_ref, side, block + pairs, 0),
            )
            for side in range(2)
        )
        stats = mix_ref[0:8, lanes], mix_ref[8:16, lanes], mix_ref[16:24, lanes]
        terms = terms_of(
            lookup(p_re, first),
            lookup(p_im, first),
            lookup(q_re, second),
            lookup(q_im, second),
            *stats,
        )
        split_into(left_ref, lanes, terms)
    sums = joined(contract(left_ref[...], hot_ref[...]))
    out = []
    low = low_half((2, LANES))
    for kind in range(3):

        def rows(start):
            return sums[start : start + 4, 0:LANES] + sums[start + 4 : start + 8, LANES:]

        p, q = rows(kind * 8), rows(24 + kind * 8)
        p = jnp.concatenate([p[0:1] + p[1:2], p[2:3] + p[3:4]], axis=0)
        q = q[0:2] + q[2:4]
        value = p + half_roll(q)
        out.append(jnp.where(low, value, half_roll(value)))
    return out


def time_kernel(
    scale,
    step,
    data_ref,
    parts_ref,
    mine_ref,
    hot_ref,
    gain_ref,
    bands_ref,
    delay_ref,
    z_ref,
    x_ref,
    send_ref,
    left_ref,
    *scratch,
):
    summed = jnp.sum(parts_ref[...].reshape(8, 16, LANES), axis=0)
    weight = 1.0 / (summed * scale + EPSILON)
    gain = gain_ref[...]
    hr, hi = band_chain(bands_ref[...], delay_ref[...], x_ref[0, 0], step)
    outer = packed_sources(gain[0:2], gain[2:4])
    sources = [
        packed_sources(
            jnp.concatenate([hr[k : k + 1], hr[8 + k : 9 + k]], axis=0),
            jnp.concatenate([hi[k : k + 1], hi[8 + k : 9 + k]], axis=0),
        )
        for k in range(8)
    ]
    for inner in range(2):
        outer_pr, outer_pi, outer_qr, outer_qi = packed_lookup(outer, mine_ref, inner)
        total = None
        for k in range(8):
            slots = scratch[3 * ((2 * k + inner) % 4) : 3 * ((2 * k + inner) % 4) + 3]
            cr, ci, power = packed_stats(
                data_ref, cell_base(k, inner), weight[inner * 8 : inner * 8 + 8], slots
            )
            ar, ai, br, bi = packed_lookup(sources[k], mine_ref, inner)
            pr, pi = cmul(outer_pr, outer_pi, ar, ai)
            qr, qi = cmul(outer_qr, outer_qi, br, bi)
            rr = cr - (pr * qr + pi * qi) * power
            ri = ci - (pi * qr - pr * qi) * power
            left_re, left_im = conj_mul(ar, ai, *cmul(qr, qi, rr, ri))
            right_re, right_im = conj_mul(br, bi, *conj_mul(rr, ri, pr, pi))
            terms = [
                left_re,
                left_im,
                (ar * ar + ai * ai) * ((qr * qr + qi * qi) * power),
                right_re,
                right_im,
                (br * br + bi * bi) * ((pr * pr + pi * pi) * power),
            ]
            total = terms if total is None else [a + b for a, b in zip(total, terms)]
        split_into(left_ref, pl.ds(inner * LANES, LANES), jnp.concatenate(total, axis=0))
    sums = joined(contract(left_ref[...], hot_ref[...]))
    row = lax.broadcasted_iota(jnp.int32, (8, LANES), 0)
    chosen = [
        jnp.sum(jnp.where(row == z_ref[0, 0], weight[h * 8 : h * 8 + 8], 0.0), axis=0, keepdims=True)
        for h in range(2)
    ]
    copies(jnp.concatenate(antenna_rows(sums) + chosen, axis=0), send_ref)


def stepped(numerator_re, numerator_im, denominator):
    return jnp.concatenate(
        [DAMPING * numerator_re / denominator, DAMPING * numerator_im / denominator], axis=0
    )


def mix_kernel(data_ref, received_ref, index_ref, gain_ref, new_ref, mix_ref, kept_ref, *scratch):
    summed = jnp.sum(received_ref[...].reshape(64, 8, LANES), axis=0)
    gain = gain_ref[...] + stepped(summed[0:2], summed[2:4], summed[4:6])
    new_ref[...] = gain
    sources = packed_sources(gain[0:2], gain[2:4])
    pairs = index_ref.shape[0] // 16
    baselines = kept_ref.shape[1]
    for pair in range(pairs):
        folded = scratch[12 + 3 * (pair % 2) : 15 + 3 * (pair % 2)]
        for half in range(2):
            block = pair + half * pairs
            weight = received_ref[pl.ds(block // 2 * 64 + 6 + block % 2, 8, stride=8), :]
            width = min(LANES, baselines - block * LANES)
            kept_ref[:, pl.ds(block * LANES, width)] = weight[:, 0:width]
            slot = (2 * pair + half) % 4
            cr, ci, power = packed_stats(
                data_ref,
                cell_base(block // 2, block % 2),
                weight,
                scratch[3 * slot : 3 * slot + 3],
            )
            pr, pi, qr, qi = packed_lookup(sources, index_ref, block)
            er, ei = conj_mul(pr, pi, qr, qi)
            ar, ai = cmul(er, ei, cr, ci)
            power = (pr * pr + pi * pi) * ((qr * qr + qi * qi) * power)
            for ref, value in zip(folded, (ar, ai, power)):
                ref[pl.ds(half * 8, 8), :] = value
        lanes = pl.ds(pair * LANES, LANES)
        for slot, ref in enumerate(folded):
            mix_ref[slot * 8 : slot * 8 + 8, lanes] = (
                ref[pl.ds(0, 8, stride=2), :] + ref[pl.ds(1, 8, stride=2), :]
            )


def solve_kernel(
    mix_ref, index_ref, hot_ref, band_ref, delay_ref, x_ref, new_ref, send_ref, left_ref
):
    x = x_ref[0, 0]
    angle = TURN * delay_ref[...] * x
    kr, ki = jnp.cos(angle), jnp.sin(angle)
    band = band_ref[...]
    hr, hi = cmul(band[0:2], band[2:4], kr, ki)
    ur, ui, w = paired_sums(mix_ref, index_ref, hot_ref, hr, hi, left_ref)
    nr, ni = conj_mul(kr, ki, ur, ui)
    band = band + stepped(nr, ni, (kr * kr + ki * ki) * w)
    new_ref[...] = band
    hr, hi = cmul(band[0:2], band[2:4], kr, ki)
    ur, ui, w = paired_sums(mix_ref, index_ref, hot_ref, hr, hi, left_ref)
    turning = TURN * x
    n = turning * (hr * ui - hi * ur)
    d = (turning * turning) * ((hr * hr + hi * hi) * w)
    low = low_half((1, LANES))
    four = [jnp.where(low, p[0:1], p[1:2]) for p in (n, d, band[0:2], band[2:4])]
    copies(jnp.concatenate(four * 2, axis=0), send_ref)


def call(body, outs, operands, scratch=()):
    vmem = pl.BlockSpec(memory_space=pltpu.VMEM)
    smem = pl.BlockSpec(memory_space=pltpu.SMEM)
    return pl.pallas_call(
        body,
        out_shape=tuple(
            o if isinstance(o, jax.ShapeDtypeStruct) else jax.ShapeDtypeStruct(o, F32)
            for o in outs
        ),
        in_specs=[smem if o.shape == (1, 1) else vmem for o in operands],
        out_specs=tuple(vmem for _ in outs),
        scratch_shapes=list(scratch),
        compiler_params=pltpu.CompilerParams(vmem_limit_bytes=12 << 20),
    )(*operands)


def exchange(array, axis):
    devices = lax.axis_size(axis)
    chunks = array.reshape(devices, 1, -1)
    return lax.all_to_all(chunks, axis, 0, 0, tiled=True).reshape(array.shape)


def pair_total(array):
    for axis in ("tm_1", "tm_0"):
        array = array + lax.ppermute(array, axis, [(0, 1), (1, 0)])
    return array


def shards(
    visibilities, sky_model, gain_time, gain_band, delay_start, first_antenna, second_antenna
):
    antennas = gain_time.shape[-1]
    baselines = visibilities.shape[4]
    blocks = 2 * lax.axis_size(YX)
    padded = blocks * LANES
    times = visibilities.shape[2]
    channels = lax.axis_size(FREQ)
    z = lax.axis_index(Z)

    def offset_of(channel):
        return ((channel.astype(F32) + 0.5) / channels - 0.5).reshape(1, 1)

    x, x0 = offset_of(lax.axis_index(FREQ)), offset_of(z)
    step = lax.axis_size(Z) / channels
    z = z.astype(jnp.int32).reshape(1, 1)
    member = lax.axis_index(YX).astype(jnp.int32).reshape(1, 1)

    def ints(*shape):
        return jax.ShapeDtypeStruct(shape, jnp.int32)

    def marks(*shape):
        return jax.ShapeDtypeStruct(shape, jnp.bfloat16)

    def rows(count):
        return (count, LANES)

    (data,) = call(
        arrange_kernel,
        [rows(8 * CHUNK)],
        (visibilities.reshape(-1, baselines), sky_model.reshape(-1, baselines), gain_band),
    )
    gain, band, delay, index, hot, mine, mine_hot = call(
        table_kernel,
        [
            rows(4),
            rows(4),
            rows(2),
            ints(blocks * 8, LANES),
            marks(4 * HALF, padded // 2),
            ints(16, LANES),
            marks(2 * HALF, 2 * LANES),
        ],
        (
            first_antenna.reshape(1, -1),
            second_antenna.reshape(1, -1),
            gain_time,
            gain_band,
            delay_start,
            member,
        ),
    )
    group = exchange(data, YX)
    wide = pltpu.VMEM((144, 2 * LANES), jnp.bfloat16)
    half_wide = pltpu.VMEM((144, padded // 2), jnp.bfloat16)
    tall, short = pltpu.VMEM((32, LANES), F32), pltpu.VMEM((16, LANES), F32)
    for sweep in range(SWEEPS):
        if sweep == 0:
            power, bands = call(
                functools.partial(first_kernel, step),
                [rows(128), rows(32)],
                (group, mine, gain, delay, x0),
            )
        else:
            power, bands, delay = call(
                functools.partial(next_kernel, step),
                [rows(128), rows(32), rows(2)],
                (group, mine, gain, delay, received, z, x0),
            )
        (send,) = call(
            functools.partial(time_kernel, 1.0 / (4 * channels), step),
            [rows(512)],
            (group, exchange(power, Z), mine, mine_hot, gain, bands, delay, z, x0),
            [wide] + [tall] * 12,
        )
        outs, scratch = [rows(4), (24, padded // 2)], [tall] * 12 + [short] * 6
        if sweep < SWEEPS - 1:
            scratch = [pltpu.VMEM((times, baselines), F32)] + scratch
        else:
            outs = outs + [(times, baselines)]
        gain, mix, *kept = call(
            mix_kernel, outs, (data, exchange(send, FREQ), index, gain), scratch
        )
        band, send = call(
            solve_kernel,
            [rows(4), rows(256)],
            (pair_total(mix), index, hot, band, delay, x),
            (half_wide,),
        )
        received = exchange(send, FREQ)
    residual, delay = call(
        last_kernel,
        [(PLANES, padded), rows(2)],
        (data, index, gain, band, delay, received, x),
    )
    return (
        gain.reshape(gain_time.shape),
        band[:, :antennas].reshape(gain_band.shape),
        delay[:, :antennas],
        kept[0],
        residual[:, :baselines].reshape(visibilities.shape),
    )


def solution(mesh):
    split = Mesh(
        mesh.devices.reshape(2, 2, 4, 2, 8), ("tm_0", "tm_1", "freq_0", "freq_1", "freq_2")
    )
    placed = (
        P(None, None, TM, FREQ, None),
        P(None, None, TM, FREQ, None),
        P(None, None, TM, None),
        P(None, None, FREQ, None),
        P(),
        P(),
        P(),
    )
    return jax.shard_map(
        shards,
        mesh=split,
        in_specs=placed,
        out_specs=(
            P(None, None, TM, None),
            P(None, None, FREQ, None),
            P(),
            P(TM, None),
            P(None, None, TM, FREQ, None),
        ),
        check_vma=False,
    )
```

```python
import functools
import math

import jax
import jax.numpy as jnp
from jax import lax
from jax.experimental import pallas as pl
from jax.experimental.pallas import tpu as pltpu
from jax.sharding import Mesh
from jax.sharding import PartitionSpec as P

SWEEPS = 2
TURN = 2.0 * math.pi
DAMPING = 0.5
EPSILON = 1e-06
LANES = 128
HALF = 64
PLANES = 64
CHUNK = 4 * PLANES + 8
CHANNELS = 64
DEEP = 8
FREQ = ("freq_0", "freq_1", "freq_2")
TM = ("tm_0", "tm_1")
YX = ("freq_0", "freq_1")
Z = "freq_2"
F32 = jnp.float32


def half_roll(array):
    return pltpu.roll(array, HALF, 1)


def low_half(shape):
    return lax.broadcasted_iota(jnp.int32, shape, 1) < HALF


def cmul(ar, ai, br, bi):
    return ar * br - ai * bi, ar * bi + ai * br


def conj_mul(ar, ai, br, bi):
    return ar * br + ai * bi, ar * bi - ai * br


def chain(gain, band, delay, x):
    angle = TURN * delay * x
    kr, ki = jnp.cos(angle), jnp.sin(angle)
    hr, hi = cmul(band[0:2], band[2:4], kr, ki)
    gr, gi = cmul(gain[0:2], gain[2:4], hr, hi)
    return (kr, ki), (hr, hi), (gr, gi)


def fill(row):
    return jnp.broadcast_to(row, (8, LANES))


def index_rows(index_ref, side, block, offset):
    return fill(index_ref[block * 8 + side : block * 8 + side + 1, :]) + offset


def lookup(source, index):
    return jnp.take_along_axis(source, index, axis=1)


def cell_base(chunk, inner):
    return chunk * CHUNK + inner * PLANES


def parts_of(data_ref, base, c):
    return tuple(
        data_ref[pl.ds(base + kind * 2 * PLANES + part * 32 + c * 8, 8), :]
        for kind in range(2)
        for part in range(2)
    )


def residual_of(data_ref, base, left, right):
    for c in range(4):
        (pr, pi), (qr, qi) = left[c // 2], right[c % 2]
        cr, ci = pr * qr + pi * qi, pi * qr - pr * qi
        vr, vi, sr, si = parts_of(data_ref, base, c)
        mr, mi = cmul(cr, ci, sr, si)
        yield c, vr - mr, vi - mi


def time_offset():
    return jnp.where(lax.broadcasted_iota(jnp.int32, (8, LANES), 0) >= 4, HALF, 0)


def offset_of(channel):
    return (channel.astype(F32) + 0.5) * (1.0 / CHANNELS) - 0.5


def own_offset(own_ref):
    return offset_of(own_ref[0, 0])


def depth(own_ref):
    return lax.rem(own_ref[0, 0], DEEP)


def stacked(pair):
    return jnp.concatenate([fill(pair[0:1]), fill(pair[1:2])], axis=0)


def band_chain(bands, delay, x0, step):
    row = lax.broadcasted_iota(jnp.int32, (16, LANES), 0) % 8
    x = x0 + step * row.astype(F32)
    angle = TURN * stacked(delay) * x
    return cmul(bands[0:16], bands[16:32], jnp.cos(angle), jnp.sin(angle))


def noise_into(data_ref, mine_ref, gain, bands, delay, x0, step, power_ref):
    hr, hi = band_chain(bands, delay, x0, step)
    gr, gi = cmul(stacked(gain[0:2]), stacked(gain[2:4]), hr, hi)
    offset = time_offset()
    index = [[index_rows(mine_ref, side, inner, offset) for side in range(2)] for inner in range(2)]
    totals = [None, None]
    for k in range(8):
        sources = [
            (fill(gr[a * 8 + k : a * 8 + k + 1]), fill(gi[a * 8 + k : a * 8 + k + 1]))
            for a in range(2)
        ]
        for inner in range(2):
            left, right = (
                [(lookup(re, at), lookup(im, at)) for re, im in sources] for at in index[inner]
            )
            for _, rr, ri in residual_of(data_ref, cell_base(k, inner), left, right):
                term = rr * rr + ri * ri
                totals[inner] = term if totals[inner] is None else totals[inner] + term
    copies(jnp.concatenate(totals, axis=0), power_ref)


def delay_step(received_ref, delay):
    summed = jnp.sum(received_ref[...].reshape(32, 8, LANES), axis=0)
    summed = summed[0:4] + summed[4:8]
    step = DAMPING * summed[0:1] / summed[1:2]
    low = low_half((1, LANES))
    turned = half_roll(jnp.broadcast_to(step, (8, LANES)))[0:1]
    both = jnp.concatenate([jnp.where(low, step, turned), jnp.where(low, turned, step)], axis=0)
    return delay + both


def side_by_side(left, right):
    return jnp.concatenate([left, right], axis=1)


def arrange_kernel(v_ref, s_ref, *refs):
    data_ref = refs[6]
    tables(*refs[:6], *refs[7:])
    baselines = v_ref.shape[1]
    band = own_band(refs[3])
    for chunk in range(8):
        for inner in range(2):
            at = (2 * chunk + inner) * LANES
            end = min(at + LANES, baselines)
            for kind, ref in enumerate((v_ref, s_ref)):
                value = ref[:, at:end]
                if end < at + LANES:
                    value = side_by_side(value, jnp.zeros((PLANES, at + LANES - end), F32))
                data_ref[pl.ds(cell_base(chunk, inner) + kind * 2 * PLANES, PLANES), :] = value
        data_ref[pl.ds(chunk * CHUNK + 4 * PLANES, 8), :] = jnp.concatenate([band, band], axis=0)


def own_band(channel_ref):
    parts = [(part, a) for part in range(2) for a in range(2)]
    band = jnp.concatenate([channel_ref[p, a] for p, a in parts], axis=0)
    return side_by_side(band, band)


def tables(
    first_ref,
    second_ref,
    time_ref,
    channel_ref,
    start_ref,
    own_ref,
    gain_ref,
    band_ref,
    delay_ref,
    index_ref,
    hot_ref,
    mine_ref,
    mine_hot_ref,
):
    parts = [(part, a) for part in range(2) for a in range(2)]
    gain_ref[...] = jnp.concatenate(
        [side_by_side(time_ref[p, a, 0:1], time_ref[p, a, 1:2]) for p, a in parts], axis=0
    )
    band_ref[...] = own_band(channel_ref)
    delay_ref[...] = side_by_side(start_ref[...], start_ref[...])
    baselines = first_ref.shape[1]
    blocks = index_ref.shape[0] // 8
    for block in range(blocks):
        at, end = block * LANES, min((block + 1) * LANES, baselines)
        rows = []
        for ref in (first_ref, second_ref):
            row = ref[0:1, at:end]
            if end < at + LANES:
                row = side_by_side(row, jnp.zeros((1, at + LANES - end), jnp.int32))
            rows.append(row)
        index_ref[pl.ds(block * 8, 8), :] = jnp.concatenate(rows * 4, axis=0)
    number = lax.broadcasted_iota(jnp.int32, (HALF, LANES), 0)

    def marks(ref, block, side):
        row = ref[block * 8 + side : block * 8 + side + 1, :]
        same = jnp.broadcast_to(row, (HALF, LANES)) == number
        return jnp.where(same, 1.0, 0.0).astype(jnp.bfloat16)

    pairs = blocks // 2
    for block in range(blocks):
        at, half = block % pairs, block // pairs
        for side in range(2):
            rows = pl.ds((half * 2 + side) * HALF, HALF)
            hot_ref[rows, pl.ds(at * LANES, LANES)] = marks(index_ref, block, side)
    mine_ref[...] = index_ref[pl.ds(pl.multiple_of(lax.div(own_ref[0, 0], DEEP) * 16, 16), 16), :]
    for inner in range(2):
        for side in range(2):
            mine_hot_ref[pl.ds(side * HALF, HALF), pl.ds(inner * LANES, LANES)] = marks(
                mine_ref, inner, side
            )


def first_kernel(
    step, data_ref, mine_ref, gain_ref, delay_ref, own_ref, power_ref, bands_ref
):
    x0 = offset_of(depth(own_ref))
    at = [k * CHUNK + 4 * PLANES for k in range(8)]
    bands = jnp.concatenate(
        [data_ref[at[k] + r : at[k] + r + 1, :] for r in range(4) for k in range(8)], axis=0
    )
    bands_ref[...] = bands
    noise_into(
        data_ref, mine_ref, gain_ref[...], bands, delay_ref[...], x0, step, power_ref
    )


def next_kernel(
    step,
    data_ref,
    mine_ref,
    gain_ref,
    delay_ref,
    received_ref,
    own_ref,
    power_ref,
    bands_ref,
    new_ref,
):
    delay = delay_step(received_ref, delay_ref[...])
    new_ref[...] = delay
    z = depth(own_ref)
    re, im = [], []
    odd = z % 2 == 1
    for k in range(8):
        value = jnp.zeros((8, LANES), F32)
        for j in range(4):
            found = received_ref[pl.ds(k * 32 + j * 8, 8), :]
            value = jnp.where(z // 2 == j, found, value)
        value = jnp.where(odd, value[4:8], value[0:4])
        re.append(value[2:3])
        im.append(value[3:4])
    low = low_half((8, LANES))
    bands = []
    for rows in (re, im):
        value = jnp.concatenate(rows, axis=0)
        turned = half_roll(value)
        bands += [jnp.where(low, value, turned), jnp.where(low, turned, value)]
    bands = jnp.concatenate(bands, axis=0)
    bands_ref[...] = bands
    x0 = offset_of(z)
    noise_into(data_ref, mine_ref, gain_ref[...], bands, delay, x0, step, power_ref)


def last_kernel(
    data_ref,
    index_ref,
    gain_ref,
    band_ref,
    delay_ref,
    weight_ref,
    received_ref,
    own_ref,
    out_ref,
    time_ref,
    channel_ref,
    last_ref,
    kept_ref,
):
    delay = delay_step(received_ref, delay_ref[...])
    last_ref[...] = delay[:, 0:HALF]
    kept_ref[...] = weight_ref[...]
    gain = gain_ref[...]
    turned = half_roll(jnp.concatenate([gain, gain], axis=0))
    for row in range(4):
        part, a = row // 2, row % 2
        time_ref[part, a, 0:1] = gain[row : row + 1, 0:HALF]
        time_ref[part, a, 1:2] = turned[row : row + 1, 0:HALF]
        channel_ref[part, a] = band_ref[row : row + 1, 0:HALF]
    _, _, (gr, gi) = chain(gain_ref[...], band_ref[...], delay, own_offset(own_ref))
    offset = time_offset()
    sources = [(fill(gr[a : a + 1]), fill(gi[a : a + 1])) for a in range(2)]
    for block in range(index_ref.shape[0] // 8):
        left, right = (
            [(lookup(re, at), lookup(im, at)) for re, im in sources]
            for at in (index_rows(index_ref, side, block, offset) for side in range(2))
        )
        lanes = pl.ds(block * LANES, LANES)
        base = cell_base(block // 2, block % 2)
        for c, rr, ri in residual_of(data_ref, base, left, right):
            out_ref[pl.ds(c * 8, 8), lanes] = rr
            out_ref[pl.ds(32 + c * 8, 8), lanes] = ri


def copies(value, out_ref):
    rows = value.shape[0]
    for at in range(0, out_ref.shape[0], rows):
        out_ref[pl.ds(at, rows), :] = value


def split_into(left_ref, lanes, terms):
    high = terms.astype(jnp.bfloat16)
    rest = terms - high.astype(F32)
    middle = rest.astype(jnp.bfloat16)
    low = (rest - middle.astype(F32)).astype(jnp.bfloat16)
    left_ref[0:48, lanes] = high
    left_ref[48:96, lanes] = middle
    left_ref[96:144, lanes] = low


def joined(sums):
    return sums[0:48] + (sums[48:96] + sums[96:144])


def contract(left, right):
    return lax.dot_general(left, right, (((1,), (1,)), ((), ())), preferred_element_type=F32)


def terms_of(pr, pi, qr, qi, cr, ci, power):
    rr = cr - (pr * qr + pi * qi) * power
    ri = ci - (pi * qr - pr * qi) * power
    return jnp.concatenate(
        [
            qr * rr - qi * ri,
            qr * ri + qi * rr,
            (qr * qr + qi * qi) * power,
            pr * rr + pi * ri,
            pi * rr - pr * ri,
            (pr * pr + pi * pi) * power,
        ],
        axis=0,
    )


def packed_sources(gr, gi):
    row = lax.broadcasted_iota(jnp.int32, (8, LANES), 0)
    offset = (row % 2) * HALF
    top = row < 4
    inner = (row // 2) % 2 == 0

    def pick(mask, part):
        return jnp.where(mask, fill(part[0:1]), fill(part[1:2]))

    return pick(top, gr), pick(top, gi), pick(inner, gr), pick(inner, gi), offset


def packed_lookup(sources, index_ref, block):
    p_re, p_im, q_re, q_im, offset = sources
    first = index_rows(index_ref, 0, block, offset)
    second = index_rows(index_ref, 1, block, offset)
    return lookup(p_re, first), lookup(p_im, first), lookup(q_re, second), lookup(q_im, second)


def packed_stats(data_ref, base, weight, scratch):
    for c in range(4):
        vr, vi, sr, si = parts_of(data_ref, base, c)
        xr, xi = conj_mul(sr, si, vr, vi)
        for ref, value in zip(scratch, (xr, xi, sr * sr + si * si)):
            ref[pl.ds(c * 8, 8), :] = weight * value
    out = []
    for ref in scratch:
        parts = [ref[pl.ds(t, 8, stride=4), :] for t in range(4)]
        out.append(parts[0] + parts[1] + (parts[2] + parts[3]))
    return out


def antenna_rows(sums):
    turned = half_roll(sums)
    low_lanes = low_half((1, LANES))
    out = []
    for kind in range(3):
        made = []
        for a in range(2):
            p, q = kind * 8 + 4 * a, 24 + kind * 8 + 2 * a

            def at(array, index):
                return array[index : index + 1]

            here = at(sums, p) + at(sums, p + 2) + (at(turned, q) + at(turned, q + 4))
            there = at(turned, p + 1) + at(turned, p + 3) + (at(sums, q + 1) + at(sums, q + 5))
            made.append(jnp.where(low_lanes, here, there))
        out.append(jnp.concatenate(made, axis=0))
    return out


def paired_sums(mix_ref, index_ref, hot_ref, hr, hi, left_ref):
    row = lax.broadcasted_iota(jnp.int32, (8, LANES), 0)
    top = row < 4
    alpha, beta = (row // 2) % 2 == 0, row % 2 == 0

    def pick(mask, part):
        return jnp.where(mask, fill(part[0:1]), fill(part[1:2]))

    p_re, p_im, q_re, q_im = pick(alpha, hr), pick(alpha, hi), pick(beta, hr), pick(beta, hi)
    pairs = mix_ref.shape[1] // LANES
    for block in range(pairs):
        lanes = pl.ds(block * LANES, LANES)
        first, second = (
            jnp.where(
                top,
                index_rows(index_ref, side, block, 0),
                index_rows(index_ref, side, block + pairs, 0),
            )
            for side in range(2)
        )
        stats = mix_ref[0:8, lanes], mix_ref[8:16, lanes], mix_ref[16:24, lanes]
        terms = terms_of(
            lookup(p_re, first),
            lookup(p_im, first),
            lookup(q_re, second),
            lookup(q_im, second),
            *stats,
        )
        split_into(left_ref, lanes, terms)
    sums = joined(contract(left_ref[...], hot_ref[...]))
    out = []
    low = low_half((2, LANES))
    for kind in range(3):

        def rows(start):
            return sums[start : start + 4, 0:LANES] + sums[start + 4 : start + 8, LANES:]

        p, q = rows(kind * 8), rows(24 + kind * 8)
        p = jnp.concatenate([p[0:1] + p[1:2], p[2:3] + p[3:4]], axis=0)
        q = q[0:2] + q[2:4]
        value = p + half_roll(q)
        out.append(jnp.where(low, value, half_roll(value)))
    return out


def time_kernel(
    scale,
    step,
    data_ref,
    parts_ref,
    mine_ref,
    hot_ref,
    gain_ref,
    bands_ref,
    delay_ref,
    own_ref,
    send_ref,
    left_ref,
    *scratch,
):
    summed = jnp.sum(parts_ref[...].reshape(8, 16, LANES), axis=0)
    weight = 1.0 / (summed * scale + EPSILON)
    gain = gain_ref[...]
    z = depth(own_ref)
    hr, hi = band_chain(bands_ref[...], delay_ref[...], offset_of(z), step)
    outer = packed_sources(gain[0:2], gain[2:4])
    sources = [
        packed_sources(
            jnp.concatenate([hr[k : k + 1], hr[8 + k : 9 + k]], axis=0),
            jnp.concatenate([hi[k : k + 1], hi[8 + k : 9 + k]], axis=0),
        )
        for k in range(8)
    ]
    for inner in range(2):
        outer_pr, outer_pi, outer_qr, outer_qi = packed_lookup(outer, mine_ref, inner)
        total = None
        for k in range(8):
            slots = scratch[3 * ((2 * k + inner) % 4) : 3 * ((2 * k + inner) % 4) + 3]
            cr, ci, power = packed_stats(
                data_ref, cell_base(k, inner), weight[inner * 8 : inner * 8 + 8], slots
            )
            ar, ai, br, bi = packed_lookup(sources[k], mine_ref, inner)
            pr, pi = cmul(outer_pr, outer_pi, ar, ai)
            qr, qi = cmul(outer_qr, outer_qi, br, bi)
            rr = cr - (pr * qr + pi * qi) * power
            ri = ci - (pi * qr - pr * qi) * power
            left_re, left_im = conj_mul(ar, ai, *cmul(qr, qi, rr, ri))
            right_re, right_im = conj_mul(br, bi, *conj_mul(rr, ri, pr, pi))
            terms = [
                left_re,
                left_im,
                (ar * ar + ai * ai) * ((qr * qr + qi * qi) * power),
                right_re,
                right_im,
                (br * br + bi * bi) * ((pr * pr + pi * pi) * power),
            ]
            total = terms if total is None else [a + b for a, b in zip(total, terms)]
        split_into(left_ref, pl.ds(inner * LANES, LANES), jnp.concatenate(total, axis=0))
    sums = joined(contract(left_ref[...], hot_ref[...]))
    row = lax.broadcasted_iota(jnp.int32, (8, LANES), 0)
    chosen = [
        jnp.sum(jnp.where(row == z, weight[h * 8 : h * 8 + 8], 0.0), axis=0, keepdims=True)
        for h in range(2)
    ]
    copies(jnp.concatenate(antenna_rows(sums) + chosen, axis=0), send_ref)


def stepped(numerator_re, numerator_im, denominator):
    return jnp.concatenate(
        [DAMPING * numerator_re / denominator, DAMPING * numerator_im / denominator], axis=0
    )


def mix_kernel(data_ref, received_ref, index_ref, gain_ref, new_ref, mix_ref, kept_ref, *scratch):
    summed = jnp.sum(received_ref[...].reshape(64, 8, LANES), axis=0)
    gain = gain_ref[...] + stepped(summed[0:2], summed[2:4], summed[4:6])
    new_ref[...] = gain
    sources = packed_sources(gain[0:2], gain[2:4])
    pairs = index_ref.shape[0] // 16
    baselines = kept_ref.shape[1]
    for pair in range(pairs):
        folded = scratch[12 + 3 * (pair % 2) : 15 + 3 * (pair % 2)]
        for half in range(2):
            block = pair + half * pairs
            weight = received_ref[pl.ds(block // 2 * 64 + 6 + block % 2, 8, stride=8), :]
            width = min(LANES, baselines - block * LANES)
            kept_ref[:, pl.ds(block * LANES, width)] = weight[:, 0:width]
            slot = (2 * pair + half) % 4
            cr, ci, power = packed_stats(
                data_ref,
                cell_base(block // 2, block % 2),
                weight,
                scratch[3 * slot : 3 * slot + 3],
            )
            pr, pi, qr, qi = packed_lookup(sources, index_ref, block)
            er, ei = conj_mul(pr, pi, qr, qi)
            ar, ai = cmul(er, ei, cr, ci)
            power = (pr * pr + pi * pi) * ((qr * qr + qi * qi) * power)
            for ref, value in zip(folded, (ar, ai, power)):
                ref[pl.ds(half * 8, 8), :] = value
        lanes = pl.ds(pair * LANES, LANES)
        for slot, ref in enumerate(folded):
            mix_ref[slot * 8 : slot * 8 + 8, lanes] = (
                ref[pl.ds(0, 8, stride=2), :] + ref[pl.ds(1, 8, stride=2), :]
            )


def solve_kernel(
    mix_ref, index_ref, hot_ref, band_ref, delay_ref, own_ref, new_ref, send_ref, left_ref
):
    x = own_offset(own_ref)
    angle = TURN * delay_ref[...] * x
    kr, ki = jnp.cos(angle), jnp.sin(angle)
    band = band_ref[...]
    hr, hi = cmul(band[0:2], band[2:4], kr, ki)
    ur, ui, w = paired_sums(mix_ref, index_ref, hot_ref, hr, hi, left_ref)
    nr, ni = conj_mul(kr, ki, ur, ui)
    band = band + stepped(nr, ni, (kr * kr + ki * ki) * w)
    new_ref[...] = band
    hr, hi = cmul(band[0:2], band[2:4], kr, ki)
    ur, ui, w = paired_sums(mix_ref, index_ref, hot_ref, hr, hi, left_ref)
    turning = TURN * x
    n = turning * (hr * ui - hi * ur)
    d = (turning * turning) * ((hr * hr + hi * hi) * w)
    low = low_half((1, LANES))
    four = [jnp.where(low, p[0:1], p[1:2]) for p in (n, d, band[0:2], band[2:4])]
    copies(jnp.concatenate(four * 2, axis=0), send_ref)


def call(body, outs, operands, scratch=()):
    vmem = pl.BlockSpec(memory_space=pltpu.VMEM)
    smem = pl.BlockSpec(memory_space=pltpu.SMEM)
    return pl.pallas_call(
        body,
        out_shape=tuple(
            o if isinstance(o, jax.ShapeDtypeStruct) else jax.ShapeDtypeStruct(o, F32)
            for o in outs
        ),
        in_specs=[smem if o.shape == (1, 1) else vmem for o in operands],
        out_specs=tuple(vmem for _ in outs),
        scratch_shapes=list(scratch),
        compiler_params=pltpu.CompilerParams(vmem_limit_bytes=12 << 20),
    )(*operands)


def exchange(array, axis):
    devices = lax.axis_size(axis)
    chunks = array.reshape(devices, 1, -1)
    return lax.all_to_all(chunks, axis, 0, 0, tiled=True).reshape(array.shape)


def pair_total(array):
    for axis in ("tm_1", "tm_0"):
        array = array + lax.ppermute(array, axis, [(0, 1), (1, 0)])
    return array


def shards(
    visibilities, sky_model, gain_time, gain_band, delay_start, first_antenna, second_antenna
):
    antennas = gain_time.shape[-1]
    baselines = visibilities.shape[4]
    blocks = 2 * lax.axis_size(YX)
    padded = blocks * LANES
    times = visibilities.shape[2]
    channels = lax.axis_size(FREQ)
    own = lax.axis_index(FREQ).astype(jnp.int32).reshape(1, 1)
    step = lax.axis_size(Z) / channels

    def ints(*shape):
        return jax.ShapeDtypeStruct(shape, jnp.int32)

    def marks(*shape):
        return jax.ShapeDtypeStruct(shape, jnp.bfloat16)

    def rows(count):
        return (count, LANES)

    data, gain, band, delay, index, hot, mine, mine_hot = call(
        arrange_kernel,
        [
            rows(8 * CHUNK),
            rows(4),
            rows(4),
            rows(2),
            ints(blocks * 8, LANES),
            marks(4 * HALF, padded // 2),
            ints(16, LANES),
            marks(2 * HALF, 2 * LANES),
        ],
        (
            visibilities.reshape(-1, baselines),
            sky_model.reshape(-1, baselines),
            first_antenna.reshape(1, -1),
            second_antenna.reshape(1, -1),
            gain_time,
            gain_band,
            delay_start,
            own,
        ),
    )
    group = exchange(data, YX)
    wide = pltpu.VMEM((144, 2 * LANES), jnp.bfloat16)
    half_wide = pltpu.VMEM((144, padded // 2), jnp.bfloat16)
    tall, short = pltpu.VMEM((32, LANES), F32), pltpu.VMEM((16, LANES), F32)
    for sweep in range(SWEEPS):
        if sweep == 0:
            power, bands = call(
                functools.partial(first_kernel, step),
                [rows(128), rows(32)],
                (group, mine, gain, delay, own),
            )
        else:
            power, bands, delay = call(
                functools.partial(next_kernel, step),
                [rows(128), rows(32), rows(2)],
                (group, mine, gain, delay, received, own),
            )
        (send,) = call(
            functools.partial(time_kernel, 1.0 / (4 * channels), step),
            [rows(512)],
            (group, exchange(power, Z), mine, mine_hot, gain, bands, delay, own),
            [wide] + [tall] * 12,
        )
        outs, scratch = [rows(4), (24, padded // 2)], [tall] * 12 + [short] * 6
        if sweep < SWEEPS - 1:
            scratch = [pltpu.VMEM((times, baselines), F32)] + scratch
        else:
            outs = outs + [(times, baselines)]
        gain, mix, *kept = call(
            mix_kernel, outs, (data, exchange(send, FREQ), index, gain), scratch
        )
        band, send = call(
            solve_kernel,
            [rows(4), rows(256)],
            (pair_total(mix), index, hot, band, delay, own),
            (half_wide,),
        )
        received = exchange(send, FREQ)
    residual, *small = call(
        last_kernel,
        [(PLANES, padded), gain_time.shape, gain_band.shape, (2, antennas), (times, baselines)],
        (data, index, gain, band, delay, kept[0], received, own),
    )
    return *small, residual[:, :baselines].reshape(visibilities.shape)


def solution(mesh):
    split = Mesh(
        mesh.devices.reshape(2, 2, 4, 2, 8), ("tm_0", "tm_1", "freq_0", "freq_1", "freq_2")
    )
    placed = (
        P(None, None, TM, FREQ, None),
        P(None, None, TM, FREQ, None),
        P(None, None, TM, None),
        P(None, None, FREQ, None),
        P(),
        P(),
        P(),
    )
    return jax.shard_map(
        shards,
        mesh=split,
        in_specs=placed,
        out_specs=(
            P(None, None, TM, None),
            P(None, None, FREQ, None),
            P(),
            P(TM, None),
            P(None, None, TM, FREQ, None),
        ),
        check_vma=False,
    )
```

```python
import functools
import math

import jax
import jax.numpy as jnp
from jax import lax
from jax.experimental import pallas as pl
from jax.experimental.pallas import tpu as pltpu
from jax.sharding import Mesh
from jax.sharding import PartitionSpec as P

SWEEPS = 2
TURN = 2.0 * math.pi
DAMPING = 0.5
EPSILON = 1e-06
LANES = 128
HALF = 64
PLANES = 64
CHUNK = 4 * PLANES + 8
CHANNELS = 64
DEEP = 8
FREQ = ("freq_0", "freq_1", "freq_2")
TM = ("tm_0", "tm_1")
YX = ("freq_0", "freq_1")
Z = "freq_2"
F32 = jnp.float32


def half_roll(array):
    return pltpu.roll(array, HALF, 1)


def low_half(shape):
    return lax.broadcasted_iota(jnp.int32, shape, 1) < HALF


def cmul(ar, ai, br, bi):
    return ar * br - ai * bi, ar * bi + ai * br


def conj_mul(ar, ai, br, bi):
    return ar * br + ai * bi, ar * bi - ai * br


def chain(gain, band, delay, x):
    angle = TURN * delay * x
    kr, ki = jnp.cos(angle), jnp.sin(angle)
    hr, hi = cmul(band[0:2], band[2:4], kr, ki)
    gr, gi = cmul(gain[0:2], gain[2:4], hr, hi)
    return (kr, ki), (hr, hi), (gr, gi)


def fill(row):
    return jnp.broadcast_to(row, (8, LANES))


def index_rows(index_ref, side, block, offset):
    return fill(index_ref[block * 8 + side : block * 8 + side + 1, :]) + offset


def lookup(source, index):
    return jnp.take_along_axis(source, index, axis=1)


def cell_base(chunk, inner):
    return chunk * CHUNK + inner * PLANES


def parts_of(data_ref, base, c):
    return tuple(
        data_ref[pl.ds(base + kind * 2 * PLANES + part * 32 + c * 8, 8), :]
        for kind in range(2)
        for part in range(2)
    )


def residual_of(data_ref, base, left, right):
    for c in range(4):
        (pr, pi), (qr, qi) = left[c // 2], right[c % 2]
        cr, ci = pr * qr + pi * qi, pi * qr - pr * qi
        vr, vi, sr, si = parts_of(data_ref, base, c)
        mr, mi = cmul(cr, ci, sr, si)
        yield c, vr - mr, vi - mi


def time_offset():
    return jnp.where(lax.broadcasted_iota(jnp.int32, (8, LANES), 0) >= 4, HALF, 0)


def offset_of(channel):
    return (channel.astype(F32) + 0.5) * (1.0 / CHANNELS) - 0.5


def own_offset(own_ref):
    return offset_of(own_ref[0, 0])


def depth(own_ref):
    return lax.rem(own_ref[0, 0], DEEP)


def stacked(pair):
    return jnp.concatenate([fill(pair[0:1]), fill(pair[1:2])], axis=0)


def band_chain(bands, delay, x0, step):
    row = lax.broadcasted_iota(jnp.int32, (16, LANES), 0) % 8
    x = x0 + step * row.astype(F32)
    angle = TURN * stacked(delay) * x
    return cmul(bands[0:16], bands[16:32], jnp.cos(angle), jnp.sin(angle))


def noise_into(data_ref, mine_ref, gain, bands, delay, x0, step, power_ref):
    hr, hi = band_chain(bands, delay, x0, step)
    gr, gi = cmul(stacked(gain[0:2]), stacked(gain[2:4]), hr, hi)
    offset = time_offset()
    index = [[index_rows(mine_ref, side, inner, offset) for side in range(2)] for inner in range(2)]
    totals = [None, None]
    for k in range(8):
        sources = [
            (fill(gr[a * 8 + k : a * 8 + k + 1]), fill(gi[a * 8 + k : a * 8 + k + 1]))
            for a in range(2)
        ]
        for inner in range(2):
            left, right = (
                [(lookup(re, at), lookup(im, at)) for re, im in sources] for at in index[inner]
            )
            for _, rr, ri in residual_of(data_ref, cell_base(k, inner), left, right):
                term = rr * rr + ri * ri
                totals[inner] = term if totals[inner] is None else totals[inner] + term
    copies(jnp.concatenate(totals, axis=0), power_ref)


def delay_step(received_ref, delay):
    rows = received_ref.shape[0]
    summed = jnp.sum(received_ref[...].reshape(rows // 8, 8, LANES), axis=0)
    summed = summed[0:4] + summed[4:8]
    if rows == 2 * CHANNELS:
        summed = summed[0:2] + summed[2:4]
    step = DAMPING * summed[0:1] / summed[1:2]
    low = low_half((1, LANES))
    turned = half_roll(jnp.broadcast_to(step, (8, LANES)))[0:1]
    both = jnp.concatenate([jnp.where(low, step, turned), jnp.where(low, turned, step)], axis=0)
    return delay + both


def side_by_side(left, right):
    return jnp.concatenate([left, right], axis=1)


def arrange_kernel(v_ref, s_ref, *refs):
    data_ref = refs[6]
    tables(*refs[:6], *refs[7:])
    baselines = v_ref.shape[1]
    band = own_band(refs[3])
    for chunk in range(8):
        for inner in range(2):
            at = (2 * chunk + inner) * LANES
            end = min(at + LANES, baselines)
            for kind, ref in enumerate((v_ref, s_ref)):
                value = ref[:, at:end]
                if end < at + LANES:
                    value = side_by_side(value, jnp.zeros((PLANES, at + LANES - end), F32))
                data_ref[pl.ds(cell_base(chunk, inner) + kind * 2 * PLANES, PLANES), :] = value
        data_ref[pl.ds(chunk * CHUNK + 4 * PLANES, 8), :] = jnp.concatenate([band, band], axis=0)


def own_band(channel_ref):
    parts = [(part, a) for part in range(2) for a in range(2)]
    band = jnp.concatenate([channel_ref[p, a] for p, a in parts], axis=0)
    return side_by_side(band, band)


def tables(
    first_ref,
    second_ref,
    time_ref,
    channel_ref,
    start_ref,
    own_ref,
    gain_ref,
    band_ref,
    delay_ref,
    index_ref,
    hot_ref,
    mine_ref,
    mine_hot_ref,
):
    parts = [(part, a) for part in range(2) for a in range(2)]
    gain_ref[...] = jnp.concatenate(
        [side_by_side(time_ref[p, a, 0:1], time_ref[p, a, 1:2]) for p, a in parts], axis=0
    )
    band_ref[...] = own_band(channel_ref)
    delay_ref[...] = side_by_side(start_ref[...], start_ref[...])
    baselines = first_ref.shape[1]
    blocks = index_ref.shape[0] // 8
    for block in range(blocks):
        at, end = block * LANES, min((block + 1) * LANES, baselines)
        rows = []
        for ref in (first_ref, second_ref):
            row = ref[0:1, at:end]
            if end < at + LANES:
                row = side_by_side(row, jnp.zeros((1, at + LANES - end), jnp.int32))
            rows.append(row)
        index_ref[pl.ds(block * 8, 8), :] = jnp.concatenate(rows * 4, axis=0)
    number = lax.broadcasted_iota(jnp.int32, (HALF, LANES), 0)

    def marks(ref, block, side):
        row = ref[block * 8 + side : block * 8 + side + 1, :]
        same = jnp.broadcast_to(row, (HALF, LANES)) == number
        return jnp.where(same, 1.0, 0.0).astype(jnp.bfloat16)

    pairs = blocks // 2
    for block in range(blocks):
        at, half = block % pairs, block // pairs
        for side in range(2):
            rows = pl.ds((half * 2 + side) * HALF, HALF)
            hot_ref[rows, pl.ds(at * LANES, LANES)] = marks(index_ref, block, side)
    mine_ref[...] = index_ref[pl.ds(pl.multiple_of(lax.div(own_ref[0, 0], DEEP) * 16, 16), 16), :]
    for inner in range(2):
        for side in range(2):
            mine_hot_ref[pl.ds(side * HALF, HALF), pl.ds(inner * LANES, LANES)] = marks(
                mine_ref, inner, side
            )


def first_kernel(
    step, data_ref, mine_ref, gain_ref, delay_ref, own_ref, power_ref, bands_ref
):
    x0 = offset_of(depth(own_ref))
    at = [k * CHUNK + 4 * PLANES for k in range(8)]
    bands = jnp.concatenate(
        [data_ref[at[k] + r : at[k] + r + 1, :] for r in range(4) for k in range(8)], axis=0
    )
    bands_ref[...] = bands
    noise_into(
        data_ref, mine_ref, gain_ref[...], bands, delay_ref[...], x0, step, power_ref
    )


def next_kernel(
    step,
    data_ref,
    mine_ref,
    gain_ref,
    delay_ref,
    received_ref,
    own_ref,
    power_ref,
    bands_ref,
    new_ref,
):
    delay = delay_step(received_ref, delay_ref[...])
    new_ref[...] = delay
    z = depth(own_ref)
    re, im = [], []
    odd = z % 2 == 1
    for k in range(8):
        value = jnp.zeros((8, LANES), F32)
        for j in range(4):
            found = received_ref[pl.ds(k * 32 + j * 8, 8), :]
            value = jnp.where(z // 2 == j, found, value)
        value = jnp.where(odd, value[4:8], value[0:4])
        re.append(value[2:3])
        im.append(value[3:4])
    low = low_half((8, LANES))
    bands = []
    for rows in (re, im):
        value = jnp.concatenate(rows, axis=0)
        turned = half_roll(value)
        bands += [jnp.where(low, value, turned), jnp.where(low, turned, value)]
    bands = jnp.concatenate(bands, axis=0)
    bands_ref[...] = bands
    x0 = offset_of(z)
    noise_into(data_ref, mine_ref, gain_ref[...], bands, delay, x0, step, power_ref)


def last_kernel(
    data_ref,
    index_ref,
    gain_ref,
    band_ref,
    delay_ref,
    weight_ref,
    received_ref,
    own_ref,
    out_ref,
    time_ref,
    channel_ref,
    last_ref,
    kept_ref,
):
    delay = delay_step(received_ref, delay_ref[...])
    last_ref[...] = delay[:, 0:HALF]
    kept_ref[...] = weight_ref[...]
    gain = gain_ref[...]
    turned = half_roll(jnp.concatenate([gain, gain], axis=0))
    for row in range(4):
        part, a = row // 2, row % 2
        time_ref[part, a, 0:1] = gain[row : row + 1, 0:HALF]
        time_ref[part, a, 1:2] = turned[row : row + 1, 0:HALF]
        channel_ref[part, a] = band_ref[row : row + 1, 0:HALF]
    _, _, (gr, gi) = chain(gain_ref[...], band_ref[...], delay, own_offset(own_ref))
    offset = time_offset()
    sources = [(fill(gr[a : a + 1]), fill(gi[a : a + 1])) for a in range(2)]
    for block in range(index_ref.shape[0] // 8):
        left, right = (
            [(lookup(re, at), lookup(im, at)) for re, im in sources]
            for at in (index_rows(index_ref, side, block, offset) for side in range(2))
        )
        lanes = pl.ds(block * LANES, LANES)
        base = cell_base(block // 2, block % 2)
        for c, rr, ri in residual_of(data_ref, base, left, right):
            out_ref[pl.ds(c * 8, 8), lanes] = rr
            out_ref[pl.ds(32 + c * 8, 8), lanes] = ri


def copies(value, out_ref):
    rows = value.shape[0]
    for at in range(0, out_ref.shape[0], rows):
        out_ref[pl.ds(at, rows), :] = value


def split_into(left_ref, lanes, terms):
    for at in range(0, 6, 2):
        pair = jnp.concatenate(terms[at : at + 2], axis=0)
        high = pair.astype(jnp.bfloat16)
        left_ref[at * 8 : at * 8 + 16, lanes] = high
        left_ref[48 + at * 8 : 64 + at * 8, lanes] = (pair - high.astype(F32)).astype(jnp.bfloat16)


def joined(sums):
    return sums[0:48] + sums[48:96]


def contract(left, right):
    return lax.dot_general(left, right, (((1,), (1,)), ((), ())), preferred_element_type=F32)


def terms_of(pr, pi, qr, qi, cr, ci, power):
    rr = cr - (pr * qr + pi * qi) * power
    ri = ci - (pi * qr - pr * qi) * power
    return [
        qr * rr - qi * ri,
        qr * ri + qi * rr,
        (qr * qr + qi * qi) * power,
        pr * rr + pi * ri,
        pi * rr - pr * ri,
        (pr * pr + pi * pi) * power,
    ]


def packed_sources(gr, gi):
    row = lax.broadcasted_iota(jnp.int32, (8, LANES), 0)
    offset = (row % 2) * HALF
    top = row < 4
    inner = (row // 2) % 2 == 0

    def pick(mask, part):
        return jnp.where(mask, fill(part[0:1]), fill(part[1:2]))

    return pick(top, gr), pick(top, gi), pick(inner, gr), pick(inner, gi), offset


def packed_lookup(sources, index_ref, block):
    p_re, p_im, q_re, q_im, offset = sources
    first = index_rows(index_ref, 0, block, offset)
    second = index_rows(index_ref, 1, block, offset)
    return lookup(p_re, first), lookup(p_im, first), lookup(q_re, second), lookup(q_im, second)


def packed_stats(data_ref, base, weight, scratch):
    for c in range(4):
        vr, vi, sr, si = parts_of(data_ref, base, c)
        xr, xi = conj_mul(sr, si, vr, vi)
        for ref, value in zip(scratch, (xr, xi, sr * sr + si * si)):
            ref[pl.ds(c * 8, 8), :] = weight * value
    out = []
    for ref in scratch:
        parts = [ref[pl.ds(t, 8, stride=4), :] for t in range(4)]
        out.append(parts[0] + parts[1] + (parts[2] + parts[3]))
    return out


def antenna_rows(sums):
    turned = half_roll(sums)
    low_lanes = low_half((1, LANES))
    out = []
    for kind in range(3):
        made = []
        for a in range(2):
            p, q = kind * 8 + 4 * a, 24 + kind * 8 + 2 * a

            def at(array, index):
                return array[index : index + 1]

            here = at(sums, p) + at(sums, p + 2) + (at(turned, q) + at(turned, q + 4))
            there = at(turned, p + 1) + at(turned, p + 3) + (at(sums, q + 1) + at(sums, q + 5))
            made.append(jnp.where(low_lanes, here, there))
        out.append(jnp.concatenate(made, axis=0))
    return out


def paired_sums(mix_ref, index_ref, hot_ref, hr, hi, left_ref):
    row = lax.broadcasted_iota(jnp.int32, (8, LANES), 0)
    top = row < 4
    alpha, beta = (row // 2) % 2 == 0, row % 2 == 0

    def pick(mask, part):
        return jnp.where(mask, fill(part[0:1]), fill(part[1:2]))

    p_re, p_im, q_re, q_im = pick(alpha, hr), pick(alpha, hi), pick(beta, hr), pick(beta, hi)
    pairs = mix_ref.shape[1] // LANES
    for block in range(pairs):
        lanes = pl.ds(block * LANES, LANES)
        first, second = (
            jnp.where(
                top,
                index_rows(index_ref, side, block, 0),
                index_rows(index_ref, side, block + pairs, 0),
            )
            for side in range(2)
        )
        stats = mix_ref[0:8, lanes], mix_ref[8:16, lanes], mix_ref[16:24, lanes]
        terms = terms_of(
            lookup(p_re, first),
            lookup(p_im, first),
            lookup(q_re, second),
            lookup(q_im, second),
            *stats,
        )
        split_into(left_ref, lanes, terms)
    sums = joined(contract(left_ref[...], hot_ref[...]))
    out = []
    low = low_half((2, LANES))
    for kind in range(3):

        def rows(start):
            return sums[start : start + 4, 0:LANES] + sums[start + 4 : start + 8, LANES:]

        p, q = rows(kind * 8), rows(24 + kind * 8)
        p = jnp.concatenate([p[0:1] + p[1:2], p[2:3] + p[3:4]], axis=0)
        q = q[0:2] + q[2:4]
        value = p + half_roll(q)
        out.append(jnp.where(low, value, half_roll(value)))
    return out


def time_kernel(
    scale,
    step,
    data_ref,
    parts_ref,
    mine_ref,
    hot_ref,
    gain_ref,
    bands_ref,
    delay_ref,
    own_ref,
    send_ref,
    left_ref,
    *scratch,
):
    summed = jnp.sum(parts_ref[...].reshape(8, 16, LANES), axis=0)
    weight = 1.0 / (summed * scale + EPSILON)
    gain = gain_ref[...]
    z = depth(own_ref)
    hr, hi = band_chain(bands_ref[...], delay_ref[...], offset_of(z), step)
    outer = packed_sources(gain[0:2], gain[2:4])
    sources = [
        packed_sources(
            jnp.concatenate([hr[k : k + 1], hr[8 + k : 9 + k]], axis=0),
            jnp.concatenate([hi[k : k + 1], hi[8 + k : 9 + k]], axis=0),
        )
        for k in range(8)
    ]
    for inner in range(2):
        outer_pr, outer_pi, outer_qr, outer_qi = packed_lookup(outer, mine_ref, inner)
        total = None
        for k in range(8):
            slots = scratch[3 * ((2 * k + inner) % 4) : 3 * ((2 * k + inner) % 4) + 3]
            cr, ci, power = packed_stats(
                data_ref, cell_base(k, inner), weight[inner * 8 : inner * 8 + 8], slots
            )
            ar, ai, br, bi = packed_lookup(sources[k], mine_ref, inner)
            pr, pi = cmul(outer_pr, outer_pi, ar, ai)
            qr, qi = cmul(outer_qr, outer_qi, br, bi)
            rr = cr - (pr * qr + pi * qi) * power
            ri = ci - (pi * qr - pr * qi) * power
            left_re, left_im = conj_mul(ar, ai, *cmul(qr, qi, rr, ri))
            right_re, right_im = conj_mul(br, bi, *conj_mul(rr, ri, pr, pi))
            terms = [
                left_re,
                left_im,
                (ar * ar + ai * ai) * ((qr * qr + qi * qi) * power),
                right_re,
                right_im,
                (br * br + bi * bi) * ((pr * pr + pi * pi) * power),
            ]
            total = terms if total is None else [a + b for a, b in zip(total, terms)]
        split_into(left_ref, pl.ds(inner * LANES, LANES), total)
    sums = joined(contract(left_ref[...], hot_ref[...]))
    row = lax.broadcasted_iota(jnp.int32, (8, LANES), 0)
    chosen = [
        jnp.sum(jnp.where(row == z, weight[h * 8 : h * 8 + 8], 0.0), axis=0, keepdims=True)
        for h in range(2)
    ]
    copies(jnp.concatenate(antenna_rows(sums) + chosen, axis=0), send_ref)


def stepped(numerator_re, numerator_im, denominator):
    return jnp.concatenate(
        [DAMPING * numerator_re / denominator, DAMPING * numerator_im / denominator], axis=0
    )


def mix_kernel(data_ref, received_ref, index_ref, gain_ref, new_ref, mix_ref, kept_ref, *scratch):
    summed = jnp.sum(received_ref[...].reshape(64, 8, LANES), axis=0)
    gain = gain_ref[...] + stepped(summed[0:2], summed[2:4], summed[4:6])
    new_ref[...] = gain
    sources = packed_sources(gain[0:2], gain[2:4])
    pairs = index_ref.shape[0] // 16
    baselines = kept_ref.shape[1]
    for pair in range(pairs):
        folded = scratch[12 + 3 * (pair % 2) : 15 + 3 * (pair % 2)]
        for half in range(2):
            block = pair + half * pairs
            weight = received_ref[pl.ds(block // 2 * 64 + 6 + block % 2, 8, stride=8), :]
            width = min(LANES, baselines - block * LANES)
            kept_ref[:, pl.ds(block * LANES, width)] = weight[:, 0:width]
            slot = (2 * pair + half) % 4
            cr, ci, power = packed_stats(
                data_ref,
                cell_base(block // 2, block % 2),
                weight,
                scratch[3 * slot : 3 * slot + 3],
            )
            pr, pi, qr, qi = packed_lookup(sources, index_ref, block)
            er, ei = conj_mul(pr, pi, qr, qi)
            ar, ai = cmul(er, ei, cr, ci)
            power = (pr * pr + pi * pi) * ((qr * qr + qi * qi) * power)
            for ref, value in zip(folded, (ar, ai, power)):
                ref[pl.ds(half * 8, 8), :] = value
        lanes = pl.ds(pair * LANES, LANES)
        for slot, ref in enumerate(folded):
            mix_ref[slot * 8 : slot * 8 + 8, lanes] = (
                ref[pl.ds(0, 8, stride=2), :] + ref[pl.ds(1, 8, stride=2), :]
            )


def solve_kernel(
    riding, mix_ref, index_ref, hot_ref, band_ref, delay_ref, own_ref, new_ref, send_ref, left_ref
):
    x = own_offset(own_ref)
    angle = TURN * delay_ref[...] * x
    kr, ki = jnp.cos(angle), jnp.sin(angle)
    band = band_ref[...]
    hr, hi = cmul(band[0:2], band[2:4], kr, ki)
    ur, ui, w = paired_sums(mix_ref, index_ref, hot_ref, hr, hi, left_ref)
    nr, ni = conj_mul(kr, ki, ur, ui)
    band = band + stepped(nr, ni, (kr * kr + ki * ki) * w)
    new_ref[...] = band
    hr, hi = cmul(band[0:2], band[2:4], kr, ki)
    ur, ui, w = paired_sums(mix_ref, index_ref, hot_ref, hr, hi, left_ref)
    turning = TURN * x
    n = turning * (hr * ui - hi * ur)
    d = (turning * turning) * ((hr * hr + hi * hi) * w)
    low = low_half((1, LANES))
    sent = [n, d] + ([band[0:2], band[2:4]] if riding else [])
    sent = [jnp.where(low, part[0:1], part[1:2]) for part in sent]
    copies(jnp.concatenate(sent * (8 // len(sent)), axis=0), send_ref)


def call(body, outs, operands, scratch=()):
    vmem = pl.BlockSpec(memory_space=pltpu.VMEM)
    smem = pl.BlockSpec(memory_space=pltpu.SMEM)
    return pl.pallas_call(
        body,
        out_shape=tuple(
            o if isinstance(o, jax.ShapeDtypeStruct) else jax.ShapeDtypeStruct(o, F32)
            for o in outs
        ),
        in_specs=[smem if o.shape == (1, 1) else vmem for o in operands],
        out_specs=tuple(vmem for _ in outs),
        scratch_shapes=list(scratch),
        compiler_params=pltpu.CompilerParams(vmem_limit_bytes=12 << 20),
    )(*operands)


def exchange(array, axis):
    devices = lax.axis_size(axis)
    chunks = array.reshape(devices, 1, -1)
    return lax.all_to_all(chunks, axis, 0, 0, tiled=True).reshape(array.shape)


def pair_total(array):
    for axis in ("tm_1", "tm_0"):
        array = array + lax.ppermute(array, axis, [(0, 1), (1, 0)])
    return array


def shards(
    visibilities, sky_model, gain_time, gain_band, delay_start, first_antenna, second_antenna
):
    antennas = gain_time.shape[-1]
    baselines = visibilities.shape[4]
    blocks = 2 * lax.axis_size(YX)
    padded = blocks * LANES
    times = visibilities.shape[2]
    channels = lax.axis_size(FREQ)
    own = lax.axis_index(FREQ).astype(jnp.int32).reshape(1, 1)
    step = lax.axis_size(Z) / channels

    def ints(*shape):
        return jax.ShapeDtypeStruct(shape, jnp.int32)

    def marks(*shape):
        return jax.ShapeDtypeStruct(shape, jnp.bfloat16)

    def rows(count):
        return (count, LANES)

    data, gain, band, delay, index, hot, mine, mine_hot = call(
        arrange_kernel,
        [
            rows(8 * CHUNK),
            rows(4),
            rows(4),
            rows(2),
            ints(blocks * 8, LANES),
            marks(4 * HALF, padded // 2),
            ints(16, LANES),
            marks(2 * HALF, 2 * LANES),
        ],
        (
            visibilities.reshape(-1, baselines),
            sky_model.reshape(-1, baselines),
            first_antenna.reshape(1, -1),
            second_antenna.reshape(1, -1),
            gain_time,
            gain_band,
            delay_start,
            own,
        ),
    )
    group = exchange(data, YX)
    wide = pltpu.VMEM((96, 2 * LANES), jnp.bfloat16)
    half_wide = pltpu.VMEM((96, padded // 2), jnp.bfloat16)
    tall, short = pltpu.VMEM((32, LANES), F32), pltpu.VMEM((16, LANES), F32)
    for sweep in range(SWEEPS):
        if sweep == 0:
            power, bands = call(
                functools.partial(first_kernel, step),
                [rows(128), rows(32)],
                (group, mine, gain, delay, own),
            )
        else:
            power, bands, delay = call(
                functools.partial(next_kernel, step),
                [rows(128), rows(32), rows(2)],
                (group, mine, gain, delay, received, own),
            )
        (send,) = call(
            functools.partial(time_kernel, 1.0 / (4 * channels), step),
            [rows(512)],
            (group, exchange(power, Z), mine, mine_hot, gain, bands, delay, own),
            [wide] + [tall] * 12,
        )
        outs, scratch = [rows(4), (24, padded // 2)], [tall] * 12 + [short] * 6
        if sweep < SWEEPS - 1:
            scratch = [pltpu.VMEM((times, baselines), F32)] + scratch
        else:
            outs = outs + [(times, baselines)]
        gain, mix, *kept = call(
            mix_kernel, outs, (data, exchange(send, FREQ), index, gain), scratch
        )
        riding = sweep < SWEEPS - 1
        band, send = call(
            functools.partial(solve_kernel, riding),
            [rows(4), rows((4 if riding else 2) * channels)],
            (pair_total(mix), index, hot, band, delay, own),
            (half_wide,),
        )
        received = exchange(send, FREQ)
    residual, *small = call(
        last_kernel,
        [(PLANES, padded), gain_time.shape, gain_band.shape, (2, antennas), (times, baselines)],
        (data, index, gain, band, delay, kept[0], received, own),
    )
    return *small, residual[:, :baselines].reshape(visibilities.shape)


def solution(mesh):
    split = Mesh(
        mesh.devices.reshape(2, 2, 4, 2, 8), ("tm_0", "tm_1", "freq_0", "freq_1", "freq_2")
    )
    placed = (
        P(None, None, TM, FREQ, None),
        P(None, None, TM, FREQ, None),
        P(None, None, TM, None),
        P(None, None, FREQ, None),
        P(),
        P(),
        P(),
    )
    return jax.shard_map(
        shards,
        mesh=split,
        in_specs=placed,
        out_specs=(
            P(None, None, TM, None),
            P(None, None, FREQ, None),
            P(),
            P(TM, None),
            P(None, None, TM, FREQ, None),
        ),
        check_vma=False,
    )
```
